32 devices in a mesh: dp: 16 (over z, x, core), tensor: 2 (over y).
Axes of the slice: x: 2, y: 2, z: 4, core: 2. Of those that a mesh axis runs over, the one named last changes fastest.
Arguments:
- block_input: bfloat16 [131072, 1024], P(('dp', 'tensor')), may hold values from -6 to 6
- output_cot: bfloat16 [131072, 1024], P(('dp', 'tensor')), may hold values from -6 to 6
- segment_ids: int32 [32, 4096], P('dp'), may hold values from 0 to 15, never falling along the last dimension, each value on 1 to 1024 neighbouring positions
- routed_index: int32 [32, 512], P('dp'), may hold values from 0 to 4095, as said below
- w_query: bfloat16 [1024, 1024], P('dp', 'tensor'), may hold values from -0.1875 to 0.1875
- w_key: bfloat16 [1024, 1024], P('dp', 'tensor'), may hold values from -0.1875 to 0.1875
- w_value: bfloat16 [1024, 1024], P('dp', 'tensor'), may hold values from -0.1875 to 0.1875
- w_output: bfloat16 [1024, 1024], P('dp', 'tensor'), may hold values from -0.75 to 0.75
- w_up: bfloat16 [1024, 4096], P('dp', 'tensor'), may hold values from -0.1875 to 0.1875
- w_down: bfloat16 [1024, 4096], P('dp', 'tensor'), may hold values from -0.09375 to 0.09375
- attn_gain: bfloat16 [1024], P('dp'), may hold values from 0.099609375 to 1.8984375
- mlp_gain: bfloat16 [1024], P('dp'), may hold values from 0.099609375 to 1.8984375
- router_w: bfloat16 [1024], P('dp'), may hold values from -0.1875 to 0.1875
Outputs:
- block_output: bfloat16 [131072, 1024], P(('dp', 'tensor'))
- block_grad: bfloat16 [131072, 1024], P(('dp', 'tensor'))
- grad_w_query: float32 [1024, 1024], P('dp', 'tensor')
- grad_w_key: float32 [1024, 1024], P('dp', 'tensor')
- grad_w_value: float32 [1024, 1024], P('dp', 'tensor')
- grad_w_output: float32 [1024, 1024], P('dp', 'tensor')
- grad_w_up: float32 [1024, 4096], P('dp', 'tensor')
- grad_w_down: float32 [1024, 4096], P('dp', 'tensor')
- grad_attn_gain: float32 [1024], P('dp')
- grad_mlp_gain: float32 [1024], P('dp')
- grad_router_w: float32 [1024], P('dp')
The draws below stay inside these ranges and needn't reach their ends.
Inputs may be any that keep to these rules, and one draw needn't show every extreme that they name: `routed_index`: each row lists 512 different positions of its sequence in rising order, always 0 and 4095 among them.
All inputs are finite; a program needn't handle non-finite values.
Results may differ from the reference program's by a relative error of at most 0.011.
Values may be sent and summed in bfloat16 or wider, within the bound.
No kernel may reach another device: no remote copies, remote signals or barrier semaphores. Data moves between devices by JAX's collectives and lax.ppermute only.
A program may use at most 192 MiB of HBM per device.

```python
import math
import jax
import jax.numpy as jnp
import numpy as np
from jax import lax

D = 1024
HEADS = 16
HEAD_DIM = 64
FF = 4096
SEQ = 4096
ROUTED = 512
DOCS = 16
DOC_MOST = 1024
SEQUENCES = 32
TOKENS = 131072


def draw_routed_index(key, part):
    row_keys = jax.random.split(key, SEQUENCES)

    def one_row(row_key):
        chosen = jax.random.permutation(row_key, SEQ - 2)[:ROUTED - 2].astype(jnp.int32) + 1
        result_row = jnp.concatenate([jnp.zeros((1,), jnp.int32), chosen, jnp.full((1,), SEQ - 1, jnp.int32)])
        return jnp.sort(result_row)
    return jax.vmap(one_row)(row_keys)


def raised(entries, key, source, target, blocks, factor):
    def block_of(axis_at):
        return (jnp.arange(entries.shape[axis_at]) // (entries.shape[axis_at] // blocks)).reshape((-1,) + (1,) * (entries.ndim - 1 - axis_at))

    one_side = jax.random.permutation(key, blocks)[block_of(target)]
    other_side = (block_of(target) + blocks // 2) % blocks
    return jnp.where((block_of(source) == one_side) | (block_of(source) == other_side), factor * entries, entries)


def levels(rng, dims, cuts, least, largest):
    factor_of = 1.0
    for axis_at, parts in cuts:
        steps = jax.random.uniform(jax.random.fold_in(jax.random.fold_in(rng, 6), axis_at), (parts,), jnp.float32, least / len(cuts), largest / len(cuts))
        factor_of = factor_of * jnp.repeat(jnp.exp(steps), dims[axis_at] // parts).reshape((-1,) + (1,) * (len(dims) - 1 - axis_at))
    return factor_of


def length_profile(amount, total, most, skew):
    portions = [(1 << 20) // math.isqrt(grade ** skew) + 1 for grade in range(2, amount + 1)]
    rest, holding = total - most - (amount - 1), [1] * (amount - 1)
    while rest > 0:
        free = [i for i in range(amount - 1) if holding[i] < most]
        mass, remaining = sum([portions[i] for i in free]), rest
        for i in free:
            more = min(most - holding[i], max(1, remaining * portions[i] // mass), rest)
            holding[i] = holding[i] + more
            rest = rest - more
    return np.array([most] + holding)


def ragged_sizes(stream_key, count, total, reach, slope):
    if count == 2:
        one = jax.random.randint(stream_key, (), max(1, total - reach), min(reach, total - 1) + 1)
        return jnp.stack([one, total - one])
    lengths = jnp.asarray(length_profile(count, total, reach, slope), jnp.int32)
    twos = (count - 1) // 2
    giver, taker = lengths[1:1 + 2 * twos:2], lengths[2:2 + 2 * twos:2]
    margin = jnp.minimum(giver - 1, reach - taker)
    shifted = jax.random.randint(jax.random.fold_in(stream_key, 1), (twos,), 0, 1 << 20) % (margin + 1)
    lengths = lengths.at[1:1 + 2 * twos:2].set(giver - shifted).at[2:2 + 2 * twos:2].set(taker + shifted)
    return lengths[jax.random.permutation(jax.random.fold_in(stream_key, 2), count)]


def centred(own_key, shape, width, most, cuts=(), held_as=jnp.bfloat16):
    level = levels(own_key, shape, cuts, -0.22, 0.18) if cuts else 1.0
    entries = jax.random.normal(own_key, shape, jnp.float32) * width * level
    return jnp.minimum(jnp.maximum(entries, -most), most).astype(held_as)


def heavy_noise(key, extent, scale, most, shards, heavy, kind=jnp.bfloat16):
    drawn = scale * jax.random.normal(key, extent, jnp.float32)
    if shards:
        drawn = drawn * levels(key, extent, shards, -0.22, 0.18)
    return jnp.clip(raised(drawn, jax.random.fold_in(key, 3), *heavy), -most, most).astype(kind)


def setup_inputs(seed: int = 0) -> dict:
    key_of = jax.random.split(jax.random.key(seed), 14)
    block_input = centred(key_of[0], (TOKENS, D), 1.0, 6.0, ((0, 32),))
    output_cot = heavy_noise(key_of[1], (TOKENS, D), 1.0, 6.0, ((0, 32),), (0, 1, 32, 2.75))
    segment_ids = jax.vmap(lambda own: jnp.searchsorted(jnp.cumsum(ragged_sizes(own, DOCS, SEQ, DOC_MOST, 2)), jnp.arange(SEQ), side="right"))(jax.random.split(key_of[2], SEQUENCES)).reshape((SEQUENCES, SEQ)).astype(jnp.int32)
    routed_index = draw_routed_index(jax.random.fold_in(key_of[13], 71), 0)
    w_query = centred(key_of[4], (D, D), D ** -0.5, 0.1875, ((0, 16), (1, 2)))
    w_key = centred(key_of[5], (D, D), D ** -0.5, 0.1875, ((0, 16), (1, 2)))
    w_value = centred(key_of[6], (D, D), D ** -0.5, 0.1875, ((0, 16), (1, 2)))
    w_output = centred(key_of[7], (D, D), (D // 16) ** -0.5, 0.75, ((0, 16), (1, 2)))
    w_up = centred(key_of[8], (D, FF), D ** -0.5, 0.1875, ((0, 16), (1, 2)))
    w_down = centred(key_of[9], (D, FF), FF ** -0.5, 0.09375, ((0, 16), (1, 2)))
    attn_gain = jnp.clip(1.0 + 0.18 * jax.random.normal(key_of[10], (D,), jnp.float32), 0.099609375, 1.8984375).astype(jnp.bfloat16)
    mlp_gain = jnp.clip(1.0 + 0.18 * jax.random.normal(key_of[11], (D,), jnp.float32), 0.099609375, 1.8984375).astype(jnp.bfloat16)
    router_w = centred(key_of[12], (D,), D ** -0.5, 0.1875, ((0, 16),))
    return {"block_input": block_input, "output_cot": output_cot, "segment_ids": segment_ids, "routed_index": routed_index, "w_query": w_query, "w_key": w_key, "w_value": w_value, "w_output": w_output, "w_up": w_up, "w_down": w_down, "attn_gain": attn_gain, "mlp_gain": mlp_gain, "router_w": router_w}


EPSILON = 1e-05
HIGH = lax.Precision.HIGHEST

@jax.custom_vjp
def low(v):
    return lax.optimization_barrier(v.astype(jnp.bfloat16)).astype(jnp.float32)

@jax.custom_vjp
def low_back(v):
    return v

def low_keep(v):
    return (low(v), None)

def low_pass(kept, grad):
    return (grad,)

def back_keep(v):
    return (v, None)

def back_low(kept, grad):
    return (low(grad),)
low.defvjp(low_keep, low_pass)
low_back.defvjp(back_keep, back_low)

def matmul(left, right):
    return jnp.dot(left, right, precision=HIGH, preferred_element_type=jnp.float32)

def rms_norm(values, gain):
    scale = lax.rsqrt(lax.optimization_barrier(jnp.mean(values * values, axis=-1, keepdims=True)) + EPSILON)
    return values * scale * gain

def sequence_forward(seq_input, segments, positions, w_query, w_key, w_value, w_output, w_up, w_down, attn_gain, mlp_gain, router_w):
    routed_rows = seq_input[positions]
    normed_attn = low(rms_norm(routed_rows, attn_gain))
    query = low(low_back(matmul(normed_attn, w_query))).reshape(ROUTED, HEADS, HEAD_DIM)
    keyed = low(low_back(matmul(normed_attn, w_key))).reshape(ROUTED, HEADS, HEAD_DIM)
    valued = low(low_back(matmul(normed_attn, w_value))).reshape(ROUTED, HEADS, HEAD_DIM)
    seg_routed = segments[positions]
    allowed = (seg_routed[:, None] == seg_routed[None, :]) & (positions[None, :] <= positions[:, None])
    scores = jnp.einsum('qhd,khd->hqk', query, keyed, precision=HIGH) * HEAD_DIM ** (-0.5)
    scores = low_back(jnp.where(allowed[None], scores, -1e+30))
    probs = low(jax.nn.softmax(scores, axis=-1))
    attended = jnp.einsum('hqk,khd->qhd', probs, valued, precision=HIGH).reshape(ROUTED, D)
    attended = low(low_back(attended))
    branch_attn = low_back(matmul(attended, w_output.T))
    middle = routed_rows + branch_attn
    normed_mlp = low(rms_norm(middle, mlp_gain))
    hidden_pre = low_back(matmul(normed_mlp, w_up))
    hidden_act = low(jax.nn.gelu(hidden_pre, approximate=True))
    branch_mlp = low_back(matmul(hidden_act, w_down.T))
    gate = jax.nn.sigmoid(matmul(routed_rows, router_w))
    updated = routed_rows + gate[:, None] * (branch_attn + branch_mlp)
    return seq_input.at[positions].set(updated)

def reference(block_input, output_cot, segment_ids, routed_index, w_query, w_key, w_value, w_output, w_up, w_down, attn_gain, mlp_gain, router_w):
    weights = tuple((weight.astype(jnp.float32) for weight in (w_query, w_key, w_value, w_output, w_up, w_down, attn_gain, mlp_gain, router_w)))
    inputs = block_input.astype(jnp.float32).reshape(SEQUENCES, SEQ, D)
    cotangents = output_cot.astype(jnp.float32).reshape(SEQUENCES, SEQ, D)

    def one_sequence(totals, sequence_items):
        seq_input, seq_cot, segments, positions = sequence_items

        def forward(seq_values, *params):
            return sequence_forward(seq_values, segments, positions, *params)
        result, pullback = jax.vjp(forward, seq_input, *weights)
        gradients = pullback(seq_cot)
        new_totals = tuple((total + grad for total, grad in zip(totals, gradients[1:])))
        return (new_totals, (result.astype(jnp.bfloat16), gradients[0].astype(jnp.bfloat16)))
    zero_grads = tuple((jnp.zeros(weight.shape, jnp.float32) for weight in weights))
    totals, (outputs, input_grads) = lax.scan(one_sequence, zero_grads, (inputs, cotangents, segment_ids, routed_index))
    return (outputs.reshape(TOKENS, D), input_grads.reshape(TOKENS, D), totals[0], totals[1], totals[2], totals[3], totals[4], totals[5], totals[6], totals[7], totals[8])
```

```python
from functools import partial

import jax
import jax.numpy as jnp
from jax import lax
from jax.experimental import pallas as pl
from jax.experimental.pallas import tpu as pltpu
from jax.sharding import PartitionSpec as P

HEAD_DIM = 64
EPSILON = 1e-05
HIGH = lax.Precision.HIGHEST
DOCS = 16
LINE = 8


def rms_norm(values, gain):
    scale = lax.rsqrt(jnp.mean(values * values, axis=-1, keepdims=True) + EPSILON)
    return values * scale * gain


def plain_dot(left, right):
    return jnp.dot(left, right, preferred_element_type=jnp.float32)


def contract_rows(left, right):
    return lax.dot_general(
        left, right, (((0,), (0,)), ((), ())), preferred_element_type=jnp.float32
    )


def contract_last(left, right):
    return lax.dot_general(
        left, right, (((1,), (1,)), ((), ())), preferred_element_type=jnp.float32
    )


class Links:
    def __init__(self):
        self.count = lax.axis_size("dp")
        self.rank = lax.axis_index("dp")
        self.side = lax.axis_index("tensor")
        self.core = self.rank % 2
        self.cross = (self.rank // 2) % 2
        self.lines = []
        rest, stride = self.count // 4, 4
        while rest > 1:
            size = min(rest, LINE)
            self.lines.append((size, stride))
            rest, stride = rest // size, stride * size
        self.chips = self.count // 4

    def ids(self):
        return jnp.stack([self.core, self.cross, self.side]).astype(jnp.int32)

    def swap(self, values, kind):
        if kind == "side":
            return lax.ppermute(values, "tensor", [(0, 1), (1, 0)])
        bit = 1 if kind == "core" else 2
        return lax.ppermute(values, "dp", [(i, i ^ bit) for i in range(self.count)])

    def shift(self, values, size, stride, step):
        pairs = []
        for i in range(self.count):
            at = (i // stride) % size + step
            if 0 <= at < size:
                pairs.append((i, i + step * stride))
        return lax.ppermute(values, "dp", pairs)

    def gather_lines(self, values):
        inner = values.shape
        values = values[None]
        for size, stride in self.lines:
            at = (self.rank // stride) % size
            lower, upper = [], []
            low = high = values
            for _ in range(size - 1):
                low = self.shift(low, size, stride, 1)
                high = self.shift(high, size, stride, -1)
                lower.insert(0, low)
                upper.append(high)
            joined = jnp.concatenate(lower + [values] + upper, axis=0)
            held = values.shape[0]
            values = lax.dynamic_slice_in_dim(joined, (size - 1 - at) * held, size * held, 0)
        return values.reshape((self.chips,) + inner)

    def gather(self, values, order):
        found = {(0, 0, 0): self.gather_lines(values)}
        places = {"core": 0, "cross": 1, "side": 2}
        for kind in order:
            for key in list(found):
                other = list(key)
                other[places[kind]] = 1
                found[tuple(other)] = self.swap(found[key], kind)
        return found

    def scatter_lines(self, values, wide=False):
        inner = values.shape[1:]
        kept = values.dtype
        for size, stride in reversed(self.lines):
            at = (self.rank // stride) % size
            held = values.shape[0] // size
            blank = jnp.zeros(((size - 1) * held,) + inner, values.dtype)
            padded = jnp.concatenate([blank, values, blank], axis=0)

            def part(off):
                return lax.dynamic_slice_in_dim(padded, (size - 1 + at + off) * held, held, 0)

            low, high = part(size - 1), part(1 - size)
            for step in range(size - 1, 0, -1):
                low = self.shift(low, size, stride, 1)
                high = self.shift(high, size, stride, -1)
                if step > 1:
                    low = low.astype(jnp.float32) + part(step - 1).astype(jnp.float32)
                    high = high.astype(jnp.float32) + part(1 - step).astype(jnp.float32)
                    low, high = low.astype(kept), high.astype(kept)
            total = part(0).astype(jnp.float32) + low.astype(jnp.float32) + high.astype(jnp.float32)
            values = total if stride == 4 else total.astype(kept)
        return values[0]

    def scatter(self, parts, order):
        places = {"core": 0, "cross": 1, "side": 2}
        for kind in order:
            place = places[kind]
            nearer = {}
            for key in parts:
                if key[place] == 0:
                    other = list(key)
                    other[place] = 1
                    got = self.swap(parts[tuple(other)], kind)
                    total = parts[key].astype(jnp.float32) + got.astype(jnp.float32)
                    nearer[key] = total.astype(got.dtype)
            parts = nearer
        return self.scatter_lines(parts[(0, 0, 0)])


KEYS = [(c, x, s) for c in (0, 1) for x in (0, 1) for s in (0, 1)]
GATHER_ORDERS = (("cross", "side", "core"), ("side", "cross", "core"))
SCATTER_ORDERS = (("core", "side", "cross"), ("core", "cross", "side"))


def place_of(ids_ref, key, chip, half, rows):
    core = jnp.bitwise_xor(ids_ref[0], key[0])
    cross = jnp.bitwise_xor(ids_ref[1], key[1])
    side = jnp.bitwise_xor(ids_ref[2], key[2])
    start = (chip * 4 + cross * 2 + core) * (2 * rows) + half * rows
    return pl.multiple_of(start, rows), side


def joined_weights(links, ids, halves, count):
    rows = halves[0][KEYS[0]].shape[1] // count
    columns = halves[0][KEYS[0]].shape[2]
    chips = links.chips
    dtype = halves[0][KEYS[0]].dtype

    def kernel(ids_ref, *refs):
        pieces, outs, sem = refs[: 2 * len(KEYS)], refs[2 * len(KEYS) : -1], refs[-1]
        copies = []
        for half in (0, 1):
            for number, key in enumerate(KEYS):
                piece = pieces[half * len(KEYS) + number]
                for chip in range(chips):
                    start, side = place_of(ids_ref, key, chip, half, rows)
                    column = pl.multiple_of(side * columns, columns)
                    for at in range(count):
                        copies.append(
                            pltpu.make_async_copy(
                                piece.at[chip, pl.ds(at * rows, rows), :],
                                outs[at].at[pl.ds(start, rows), pl.ds(column, columns)],
                                sem,
                            )
                        )
        for copy in copies:
            copy.start()
        for copy in copies:
            copy.wait()

    operands = [halves[half][key] for half in (0, 1) for key in KEYS]
    anywhere = pl.BlockSpec(memory_space=pl.ANY)
    return pl.pallas_call(
        kernel,
        out_shape=[jax.ShapeDtypeStruct((8 * chips * rows, 2 * columns), dtype)] * count,
        in_specs=[pl.BlockSpec(memory_space=pltpu.SMEM)] + [anywhere] * len(operands),
        out_specs=[anywhere] * count,
        scratch_shapes=[pltpu.SemaphoreType.DMA],
        name="join",
    )(ids, *operands)


def split_gradients(links, ids, grads):
    count = len(grads)
    chips = links.chips
    rows = grads[0].shape[0] // (8 * chips)
    columns = grads[0].shape[1] // 2

    def kernel(ids_ref, *refs):
        wholes, outs, sem = refs[:count], refs[count:-1], refs[-1]
        copies = []
        for half in (0, 1):
            for number, key in enumerate(KEYS):
                piece = outs[half * len(KEYS) + number]
                for chip in range(chips):
                    start, side = place_of(ids_ref, key, chip, half, rows)
                    column = pl.multiple_of(side * columns, columns)
                    for at in range(count):
                        copies.append(
                            pltpu.make_async_copy(
                                wholes[at].at[pl.ds(start, rows), pl.ds(column, columns)],
                                piece.at[chip, pl.ds(at * rows, rows), :],
                                sem,
                            )
                        )
        for copy in copies:
            copy.start()
        for copy in copies:
            copy.wait()

    anywhere = pl.BlockSpec(memory_space=pl.ANY)
    shape = jax.ShapeDtypeStruct((chips, count * rows, columns), grads[0].dtype)
    outs = pl.pallas_call(
        kernel,
        out_shape=[shape] * (2 * len(KEYS)),
        in_specs=[pl.BlockSpec(memory_space=pltpu.SMEM)] + [anywhere] * count,
        out_specs=[anywhere] * (2 * len(KEYS)),
        scratch_shapes=[pltpu.SemaphoreType.DMA],
        name="split",
    )(ids, *grads)
    return [
        {key: outs[half * len(KEYS) + number] for number, key in enumerate(KEYS)}
        for half in (0, 1)
    ]


def gather_weights(links, ids, shards):
    rows = shards[0].shape[0] // 2
    halves = []
    for half in (0, 1):
        share = jnp.concatenate([shard[half * rows : (half + 1) * rows] for shard in shards], axis=0)
        halves.append(links.gather(share, GATHER_ORDERS[half]))
    return joined_weights(links, ids, halves, len(shards))


def scatter_gradients(links, ids, grads):
    rows = grads[0].shape[0] // (8 * links.chips)
    halves = split_gradients(links, ids, [grad.astype(jnp.bfloat16) for grad in grads])
    sums = [links.scatter(halves[half], SCATTER_ORDERS[half]) for half in (0, 1)]
    return [
        jnp.concatenate([total[at * rows : (at + 1) * rows] for total in sums], axis=0)
        for at in range(len(grads))
    ]


def local(
    block_input,
    output_cot,
    segment_ids,
    routed_index,
    w_query,
    w_key,
    w_value,
    w_output,
    w_up,
    w_down,
    attn_gain,
    mlp_gain,
    router_w,
):
    links = Links()
    ids = links.ids()
    routed_rows = routed_index.shape[1]
    width = block_input.shape[1]
    heads = width // HEAD_DIM
    scale = HEAD_DIM ** (-0.5)

    small = jnp.stack([attn_gain, mlp_gain, router_w])
    small = links.gather_lines(small)
    other = links.swap(small, "cross")
    small = jnp.stack(
        [jnp.where(links.cross == 0, small, other), jnp.where(links.cross == 0, other, small)], axis=1
    )
    other = links.swap(small, "core")
    small = jnp.stack(
        [jnp.where(links.core == 0, small, other), jnp.where(links.core == 0, other, small)], axis=2
    )
    small = jnp.moveaxis(small, 3, 0).reshape(3, width).astype(jnp.float32)
    attn_gain_f, mlp_gain_f, router_f = small[0], small[1], small[2]

    full_query, full_key, full_value = gather_weights(links, ids, [w_query, w_key, w_value])
    (full_output,) = gather_weights(links, ids, [w_output])
    (full_up,) = gather_weights(links, ids, [w_up])
    (full_down,) = gather_weights(links, ids, [w_down])

    own_index = lax.dynamic_index_in_dim(routed_index, links.side, 0, keepdims=False)
    own_segments = lax.dynamic_index_in_dim(segment_ids, links.side, 0, keepdims=False)
    own_input = jnp.take(block_input, own_index, axis=0)
    input_float = own_input.astype(jnp.float32)
    cot_rows = jnp.take(output_cot, own_index, axis=0).astype(jnp.float32)
    firsts = jnp.sum(
        (own_segments[None, :] < jnp.arange(1, DOCS, dtype=jnp.int32)[:, None]).astype(jnp.int32), axis=1
    )
    seg_routed = jnp.sum((own_index[:, None] >= firsts[None, :]).astype(jnp.int32), axis=1)
    allowed = (seg_routed[:, None] == seg_routed[None, :]) & (own_index[None, :] <= own_index[:, None])
    allowed = allowed[None]

    def split_heads(values):
        return values.reshape(routed_rows, heads, HEAD_DIM)

    def merge_heads(values):
        return values.reshape(routed_rows, width)

    normed_attn = rms_norm(input_float, attn_gain_f).astype(jnp.bfloat16)
    gate = jax.nn.sigmoid(jnp.sum(input_float * router_f, axis=-1))
    d_branch = gate[:, None] * cot_rows
    d_mlp_low = d_branch.astype(jnp.bfloat16)

    query = split_heads(plain_dot(normed_attn, full_query).astype(jnp.bfloat16))
    keyed = split_heads(plain_dot(normed_attn, full_key).astype(jnp.bfloat16))
    valued = split_heads(plain_dot(normed_attn, full_value).astype(jnp.bfloat16))

    def make_scores():
        raw = jnp.einsum("qhd,khd->hqk", query, keyed, preferred_element_type=jnp.float32) * scale
        return jnp.where(allowed, raw, -1e30)

    scores = make_scores()
    row_max = jnp.max(scores, axis=-1, keepdims=True)
    expanded = jnp.exp(scores - row_max)
    row_total = jnp.sum(expanded, axis=-1, keepdims=True)
    probs = expanded / row_total
    log_total = row_max + jnp.log(row_total)
    probs_low = probs.astype(jnp.bfloat16)
    attended = merge_heads(
        jnp.einsum("hqk,khd->qhd", probs_low, valued, preferred_element_type=jnp.float32).astype(
            jnp.bfloat16
        )
    )
    branch_attn = contract_last(attended, full_output)
    middle = input_float + branch_attn
    normed_mlp = rms_norm(middle, mlp_gain_f).astype(jnp.bfloat16)
    hidden_pre = plain_dot(normed_mlp, full_up)
    hidden_act = jax.nn.gelu(hidden_pre, approximate=True).astype(jnp.bfloat16)
    grad_down = contract_rows(d_mlp_low, hidden_act)
    (sum_down,) = scatter_gradients(links, ids, [grad_down])

    branch_mlp = contract_last(hidden_act, full_down)
    branch_total = branch_attn + branch_mlp
    updated = input_float + gate[:, None] * branch_total
    block_output = block_input.at[own_index].set(updated.astype(jnp.bfloat16))
    d_logit = gate * (1.0 - gate) * jnp.sum(cot_rows * branch_total, axis=-1)
    d_act = plain_dot(d_mlp_low, full_down)
    unused_act, gelu_back = jax.vjp(partial(jax.nn.gelu, approximate=True), hidden_pre)
    d_pre = gelu_back(d_act)[0].astype(jnp.bfloat16)
    grad_up = contract_rows(normed_mlp, d_pre)
    (sum_up,) = scatter_gradients(links, ids, [grad_up])
    d_normed_mlp = contract_last(d_pre, full_up)
    unused_mid, norm_back_mlp = jax.vjp(rms_norm, middle, mlp_gain_f)
    d_middle, d_mlp_gain = norm_back_mlp(d_normed_mlp)
    d_attn_low = (d_branch + d_middle).astype(jnp.bfloat16)
    d_attended = split_heads(plain_dot(d_attn_low, full_output).astype(jnp.bfloat16))
    grad_output = contract_rows(d_attn_low, attended)
    (sum_output,) = scatter_gradients(links, ids, [grad_output])

    scores_again = make_scores()
    probs_again = jnp.exp(scores_again - log_total)
    probs_again_low = probs_again.astype(jnp.bfloat16)
    d_probs = jnp.einsum("qhd,khd->hqk", d_attended, valued, preferred_element_type=jnp.float32)
    row_inner = jnp.sum(probs_again * d_probs, axis=-1, keepdims=True)
    d_scores = (probs_again * (d_probs - row_inner)).astype(jnp.bfloat16)
    d_query = merge_heads(
        (jnp.einsum("hqk,khd->qhd", d_scores, keyed, preferred_element_type=jnp.float32) * scale).astype(
            jnp.bfloat16
        )
    )
    d_key = merge_heads(
        (jnp.einsum("hqk,qhd->khd", d_scores, query, preferred_element_type=jnp.float32) * scale).astype(
            jnp.bfloat16
        )
    )
    d_value = merge_heads(
        jnp.einsum("hqk,qhd->khd", probs_again_low, d_attended, preferred_element_type=jnp.float32).astype(
            jnp.bfloat16
        )
    )
    sum_query, sum_key, sum_value = scatter_gradients(
        links,
        ids,
        [
            contract_rows(normed_attn, d_query),
            contract_rows(normed_attn, d_key),
            contract_rows(normed_attn, d_value),
        ],
    )
    d_normed_attn = (
        contract_last(d_query, full_query)
        + contract_last(d_key, full_key)
        + contract_last(d_value, full_value)
    )
    unused_norm, norm_back_attn = jax.vjp(rms_norm, input_float, attn_gain_f)
    d_input_norm, d_attn_gain = norm_back_attn(d_normed_attn)
    d_router = jnp.dot(d_logit, input_float, precision=HIGH, preferred_element_type=jnp.float32)
    routed_grad = cot_rows + d_logit[:, None] * router_f + d_middle + d_input_norm
    block_grad = output_cot.at[own_index].set(routed_grad.astype(jnp.bfloat16))

    totals = jnp.stack([d_attn_gain, d_mlp_gain, d_router])
    totals = totals.reshape(3, links.chips, 2, 2, -1)
    near = lax.dynamic_index_in_dim(totals, links.core, 3, keepdims=False)
    far = lax.dynamic_index_in_dim(totals, 1 - links.core, 3, keepdims=False)
    totals = near + links.swap(far, "core")
    near = lax.dynamic_index_in_dim(totals, links.cross, 2, keepdims=False)
    far = lax.dynamic_index_in_dim(totals, 1 - links.cross, 2, keepdims=False)
    totals = near + links.swap(far, "cross")
    totals = totals + links.swap(totals, "side")
    sum_small = links.scatter_lines(jnp.moveaxis(totals, 1, 0))
    return (
        block_output,
        block_grad,
        sum_query,
        sum_key,
        sum_value,
        sum_output,
        sum_up,
        sum_down,
        sum_small[0],
        sum_small[1],
        sum_small[2],
    )


def solution(mesh):
    in_specs = (
        P(("dp", "tensor"), None),
        P(("dp", "tensor"), None),
        P("dp", None),
        P("dp", None),
        P("dp", "tensor"),
        P("dp", "tensor"),
        P("dp", "tensor"),
        P("dp", "tensor"),
        P("dp", "tensor"),
        P("dp", "tensor"),
        P("dp"),
        P("dp"),
        P("dp"),
    )
    out_specs = (
        P(("dp", "tensor"), None),
        P(("dp", "tensor"), None),
        P("dp", "tensor"),
        P("dp", "tensor"),
        P("dp", "tensor"),
        P("dp", "tensor"),
        P("dp", "tensor"),
        P("dp", "tensor"),
        P("dp"),
        P("dp"),
        P("dp"),
    )
    return jax.shard_map(local, mesh=mesh, in_specs=in_specs, out_specs=out_specs, check_vma=False)
```

```python
from functools import partial

import jax
import jax.numpy as jnp
from jax import lax
from jax.experimental import pallas as pl
from jax.experimental.pallas import tpu as pltpu
from jax.sharding import Mesh
from jax.sharding import PartitionSpec as P

HEAD_DIM = 64
EPSILON = 1e-05
DOCS = 16
PAIR = 2 * HEAD_DIM
DP = ("chips", "core")
ALL = ("tensor", "chips", "core")
SAME_CORE = ("tensor", "chips")


def rms_norm(values, gain):
    scale = lax.rsqrt(jnp.mean(values * values, axis=-1, keepdims=True) + EPSILON)
    return values * scale * gain


def plain_dot(left, right):
    return jnp.dot(left, right, preferred_element_type=jnp.float32)


def contract_rows(left, right):
    return lax.dot_general(
        left, right, (((0,), (0,)), ((), ())), preferred_element_type=jnp.float32
    )


def contract_last(left, right):
    return lax.dot_general(
        left, right, (((1,), (1,)), ((), ())), preferred_element_type=jnp.float32
    )


def fill_bias(seg_row_ref, seg_column_ref, bias_ref):
    rows = bias_ref.shape[0]
    key_at = lax.broadcasted_iota(jnp.int32, (rows, rows), 0)
    query_at = lax.broadcasted_iota(jnp.int32, (rows, rows), 1)
    same = seg_column_ref[...] == seg_row_ref[...]
    bias_ref[...] = jnp.where(same & (key_at <= query_at), 0.0, -1e30)


def lanes_of(head):
    lane = lax.broadcasted_iota(jnp.int32, (1, PAIR), 1)
    return (lane // HEAD_DIM == head).astype(jnp.bfloat16)


def attend(qkv, seg_row, seg_column):
    rows, width = qkv.shape[0], qkv.shape[1] // 3
    pairs = width // PAIR
    scale = HEAD_DIM ** (-0.5)

    def kernel(seg_row_ref, seg_column_ref, q_ref, k_ref, v_ref, out_ref, lse_ref, bias_ref):
        @pl.when(pl.program_id(0) == 0)
        def _():
            fill_bias(seg_row_ref, seg_column_ref, bias_ref)

        query, keyed, valued = q_ref[...], k_ref[...], v_ref[...]
        found = []
        for head in (0, 1):
            chosen = query * (lanes_of(head) * scale).astype(jnp.bfloat16)
            scores = contract_last(keyed, chosen) + bias_ref[...]
            top = jnp.max(scores, axis=0, keepdims=True)
            expanded = jnp.exp(scores - top)
            total = jnp.sum(expanded, axis=0, keepdims=True)
            lse_ref[head, :, :] = top + jnp.log(total)
            probs = (expanded * (1.0 / total)).astype(jnp.bfloat16)
            found.append(contract_rows(probs, valued))
        lane = lax.broadcasted_iota(jnp.int32, (1, PAIR), 1)
        out_ref[...] = jnp.where(lane < HEAD_DIM, found[0], found[1]).astype(jnp.bfloat16)

    return pl.pallas_call(
        kernel,
        grid=(pairs,),
        out_shape=[
            jax.ShapeDtypeStruct((rows, width), jnp.bfloat16),
            jax.ShapeDtypeStruct((2 * pairs, 1, rows), jnp.float32),
        ],
        in_specs=[
            pl.BlockSpec((1, rows), lambda j: (0, 0)),
            pl.BlockSpec((rows, 1), lambda j: (0, 0)),
            pl.BlockSpec((rows, PAIR), lambda j: (0, j)),
            pl.BlockSpec((rows, PAIR), lambda j: (0, pairs + j)),
            pl.BlockSpec((rows, PAIR), lambda j: (0, 2 * pairs + j)),
        ],
        out_specs=[
            pl.BlockSpec((rows, PAIR), lambda j: (0, j)),
            pl.BlockSpec((2, 1, rows), lambda j: (j, 0, 0)),
        ],
        scratch_shapes=[pltpu.VMEM((rows, rows), jnp.float32)],
        name="attend",
    )(seg_row, seg_column, qkv, qkv, qkv)


def attend_back(qkv, d_attended, lse, seg_row, seg_column):
    rows, width = qkv.shape[0], qkv.shape[1] // 3
    pairs = width // PAIR
    scale = HEAD_DIM ** (-0.5)

    def kernel(seg_row_ref, seg_column_ref, q_ref, k_ref, v_ref, d_ref, lse_ref, out_ref, bias_ref):
        step = pl.program_id(0)

        @pl.when(step == 0)
        def _():
            fill_bias(seg_row_ref, seg_column_ref, bias_ref)

        query, keyed, valued, d_out = q_ref[...], k_ref[...], v_ref[...], d_ref[...]
        scaled = query * jnp.bfloat16(scale)
        d_query, d_key, d_value = [], [], []
        for head in (0, 1):
            lanes = lanes_of(head)
            scores = contract_last(keyed, scaled * lanes) + bias_ref[...]
            probs = jnp.exp(scores - lse_ref[head, :, :])
            d_probs = contract_last(valued, d_out * lanes)
            inner = jnp.sum(probs * d_probs, axis=0, keepdims=True)
            d_scores = (probs * (d_probs - inner)).astype(jnp.bfloat16)
            d_value.append(plain_dot(probs.astype(jnp.bfloat16), d_out))
            d_key.append(plain_dot(d_scores, scaled))
            d_query.append(contract_rows(d_scores, keyed) * scale)
        lane = lax.broadcasted_iota(jnp.int32, (1, PAIR), 1)
        for at, pair in enumerate((d_query, d_key, d_value)):
            column = pl.multiple_of(at * width + step * PAIR, PAIR)
            out_ref[:, pl.ds(column, PAIR)] = jnp.where(lane < HEAD_DIM, pair[0], pair[1]).astype(
                jnp.bfloat16
            )

    return pl.pallas_call(
        kernel,
        grid=(pairs,),
        out_shape=jax.ShapeDtypeStruct((rows, 3 * width), jnp.bfloat16),
        in_specs=[
            pl.BlockSpec((1, rows), lambda j: (0, 0)),
            pl.BlockSpec((rows, 1), lambda j: (0, 0)),
            pl.BlockSpec((rows, PAIR), lambda j: (0, j)),
            pl.BlockSpec((rows, PAIR), lambda j: (0, pairs + j)),
            pl.BlockSpec((rows, PAIR), lambda j: (0, 2 * pairs + j)),
            pl.BlockSpec((rows, PAIR), lambda j: (0, j)),
            pl.BlockSpec((2, 1, rows), lambda j: (j, 0, 0)),
        ],
        out_specs=pl.BlockSpec((rows, 3 * width), lambda j: (0, 0)),
        scratch_shapes=[pltpu.VMEM((rows, rows), jnp.float32)],
        name="attend_back",
    )(seg_row, seg_column, qkv, qkv, qkv, d_attended, lse)


def swap_cores(values):
    return lax.ppermute(values, "core", [(0, 1), (1, 0)])


def reduce_grads(grads):
    chips, core = lax.axis_size("chips"), lax.axis_index("core")
    stacked = jnp.stack(grads)
    sides, width, columns = stacked.shape
    stacked = stacked.reshape(sides, chips, 2, width // (2 * chips), columns)
    kept = lax.dynamic_index_in_dim(stacked, core, 2, keepdims=False)
    sent = lax.dynamic_index_in_dim(stacked, 1 - core, 2, keepdims=False).astype(jnp.bfloat16)
    total = (kept.astype(jnp.float32) + swap_cores(sent).astype(jnp.float32)).astype(jnp.bfloat16)
    total = total.reshape(-1, columns)
    return lax.psum_scatter(total, SAME_CORE, scatter_dimension=0, tiled=True).astype(jnp.float32)


def sum_everywhere(values):
    values = values + swap_cores(values)
    values = values + lax.ppermute(values, "tensor", [(0, 1), (1, 0)])
    count, bit = lax.axis_size("chips"), 1
    while bit < count:
        values = values + lax.ppermute(values, "chips", [(i, i ^ bit) for i in range(count)])
        bit *= 2
    return values


def local(
    block_input,
    output_cot,
    segment_ids,
    routed_index,
    w_query,
    w_key,
    w_value,
    w_output,
    w_up,
    w_down,
    attn_gain,
    mlp_gain,
    router_w,
):
    side = lax.axis_index("tensor")
    sides = lax.axis_size("tensor")
    rank = lax.axis_index(DP)
    width = block_input.shape[1]
    share, heads = w_query.shape
    hidden = w_up.shape[1]

    vectors = jnp.stack([attn_gain, mlp_gain, router_w], axis=1)
    vectors = jnp.pad(vectors, ((0, 0), (0, 128 - 3)))
    near = jnp.concatenate([w_query, w_key, w_value, w_output, vectors], axis=1)
    near = lax.all_gather(near, ALL, axis=0, tiled=True).reshape(sides, width, -1)
    far = jnp.concatenate([w_up, w_down], axis=1)
    far = lax.all_gather(far, ALL, axis=0, tiled=True).reshape(sides, width, -1)
    full_qkv = [near[t, :, : 3 * heads] for t in range(sides)]
    full_output = [near[t, :, 3 * heads : 4 * heads] for t in range(sides)]
    full_up = [far[t, :, :hidden] for t in range(sides)]
    full_down = [far[t, :, hidden:] for t in range(sides)]
    small = near[0, :, 4 * heads : 4 * heads + 3].astype(jnp.float32).T
    attn_gain_f, mlp_gain_f, router_f = small[0], small[1], small[2]

    own_index = lax.dynamic_index_in_dim(routed_index, side, 0, keepdims=False)
    own_segments = lax.dynamic_index_in_dim(segment_ids, side, 0, keepdims=False)
    input_float = jnp.take(block_input, own_index, axis=0).astype(jnp.float32)
    cot_rows = jnp.take(output_cot, own_index, axis=0).astype(jnp.float32)
    firsts = jnp.sum(
        (own_segments[None, :] < jnp.arange(1, DOCS, dtype=jnp.int32)[:, None]).astype(jnp.int32), axis=1
    )
    seg_routed = jnp.sum((own_index[:, None] >= firsts[None, :]).astype(jnp.int32), axis=1)
    seg_row, seg_column = seg_routed[None, :], seg_routed[:, None]

    normed_attn = rms_norm(input_float, attn_gain_f).astype(jnp.bfloat16)
    gate = jax.nn.sigmoid(jnp.sum(input_float * router_f, axis=-1))
    d_branch = gate[:, None] * cot_rows
    d_mlp_low = d_branch.astype(jnp.bfloat16)

    qkv = [plain_dot(normed_attn, full_qkv[t]).astype(jnp.bfloat16) for t in range(sides)]
    attended, lse = zip(*[attend(qkv[t], seg_row, seg_column) for t in range(sides)])
    branch_attn = sum(contract_last(attended[t], full_output[t]) for t in range(sides))
    middle = input_float + branch_attn
    normed_mlp = rms_norm(middle, mlp_gain_f).astype(jnp.bfloat16)

    hidden_pre = [plain_dot(normed_mlp, full_up[t]) for t in range(sides)]
    hidden_act = [jax.nn.gelu(hidden_pre[t], approximate=True).astype(jnp.bfloat16) for t in range(sides)]
    d_pre = []
    for t in range(sides):
        unused_act, gelu_back = jax.vjp(partial(jax.nn.gelu, approximate=True), hidden_pre[t])
        d_pre.append(gelu_back(plain_dot(d_mlp_low, full_down[t]))[0].astype(jnp.bfloat16))
    grad_mlp = [
        jnp.concatenate(
            [contract_rows(normed_mlp, d_pre[t]), contract_rows(d_mlp_low, hidden_act[t])], axis=1
        ).astype(jnp.bfloat16)
        for t in range(sides)
    ]
    sum_mlp = reduce_grads(grad_mlp)

    d_normed_mlp = sum(contract_last(d_pre[t], full_up[t]) for t in range(sides))
    unused_mid, norm_back_mlp = jax.vjp(rms_norm, middle, mlp_gain_f)
    d_middle, d_mlp_gain = norm_back_mlp(d_normed_mlp)
    d_attn_low = (d_branch + d_middle).astype(jnp.bfloat16)
    d_qkv = []
    for t in range(sides):
        d_attended = plain_dot(d_attn_low, full_output[t]).astype(jnp.bfloat16)
        d_qkv.append(attend_back(qkv[t], d_attended, lse[t], seg_row, seg_column))
    grad_attn = [
        jnp.concatenate(
            [contract_rows(normed_attn, d_qkv[t]), contract_rows(d_attn_low, attended[t])], axis=1
        ).astype(jnp.bfloat16)
        for t in range(sides)
    ]
    sum_attn = reduce_grads(grad_attn)

    branch_mlp = sum(contract_last(hidden_act[t], full_down[t]) for t in range(sides))
    branch_total = branch_attn + branch_mlp
    updated = input_float + gate[:, None] * branch_total
    block_output = block_input.at[own_index].set(updated.astype(jnp.bfloat16))
    d_logit = gate * (1.0 - gate) * jnp.sum(cot_rows * branch_total, axis=-1)

    d_normed_attn = sum(contract_last(d_qkv[t], full_qkv[t]) for t in range(sides))
    unused_norm, norm_back_attn = jax.vjp(rms_norm, input_float, attn_gain_f)
    d_input_norm, d_attn_gain = norm_back_attn(d_normed_attn)
    d_router = jnp.sum(d_logit[:, None] * input_float, axis=0)
    routed_grad = cot_rows + d_logit[:, None] * router_f + d_middle + d_input_norm
    block_grad = output_cot.at[own_index].set(routed_grad.astype(jnp.bfloat16))

    totals = sum_everywhere(jnp.stack([d_attn_gain, d_mlp_gain, d_router]))
    own = lax.dynamic_slice_in_dim(totals, rank * share, share, axis=1)
    return (
        block_output,
        block_grad,
        sum_attn[:, :heads],
        sum_attn[:, heads : 2 * heads],
        sum_attn[:, 2 * heads : 3 * heads],
        sum_attn[:, 3 * heads :],
        sum_mlp[:, :hidden],
        sum_mlp[:, hidden:],
        own[0],
        own[1],
        own[2],
    )


def solution(mesh):
    fine = Mesh(mesh.devices.reshape(-1, 2, mesh.shape["tensor"]), ("chips", "core", "tensor"))
    token = P(("chips", "core", "tensor"), None)
    weight = P(DP, "tensor")
    in_specs = (token, token, P(DP, None), P(DP, None)) + (weight,) * 6 + (P(DP),) * 3
    out_specs = (token, token) + (weight,) * 6 + (P(DP),) * 3
    return jax.shard_map(local, mesh=fine, in_specs=in_specs, out_specs=out_specs, check_vma=False)
```

```python
from functools import partial

import jax
import jax.numpy as jnp
from jax import lax
from jax.experimental import pallas as pl
from jax.experimental.pallas import tpu as pltpu
from jax.sharding import Mesh
from jax.sharding import PartitionSpec as P


HEAD_DIM = 64
EPSILON = 1e-05
DOCS = 16
PAIR = 2 * HEAD_DIM
DP = ("chips", "core")
ALL = ("tensor", "chips", "core")
SAME_CORE = ("tensor", "chips")


def rms_norm(values, gain):
    scale = lax.rsqrt(jnp.mean(values * values, axis=-1, keepdims=True) + EPSILON)
    return values * scale * gain


def plain_dot(left, right):
    return jnp.dot(left, right, preferred_element_type=jnp.float32)


def contract_rows(left, right):
    return lax.dot_general(
        left, right, (((0,), (0,)), ((), ())), preferred_element_type=jnp.float32
    )


def contract_last(left, right):
    return lax.dot_general(
        left, right, (((1,), (1,)), ((), ())), preferred_element_type=jnp.float32
    )


def fill_bias(seg_row_ref, seg_column_ref, bias_ref):
    rows = bias_ref.shape[0]
    key_at = lax.broadcasted_iota(jnp.int32, (rows, rows), 0)
    query_at = lax.broadcasted_iota(jnp.int32, (rows, rows), 1)
    same = seg_column_ref[...] == seg_row_ref[...]
    bias_ref[...] = jnp.where(same & (key_at <= query_at), 0.0, -1e30)


def lanes_of(head):
    lane = lax.broadcasted_iota(jnp.int32, (1, PAIR), 1)
    return (lane // HEAD_DIM == head).astype(jnp.bfloat16)


def attend(qkv, seg_row, seg_column):
    rows, width = qkv.shape[0], qkv.shape[1] // 3
    pairs = width // PAIR
    scale = HEAD_DIM ** (-0.5)

    def kernel(seg_row_ref, seg_column_ref, q_ref, k_ref, v_ref, out_ref, lse_ref, bias_ref):
        @pl.when(pl.program_id(0) == 0)
        def _():
            fill_bias(seg_row_ref, seg_column_ref, bias_ref)

        query, keyed, valued = q_ref[...], k_ref[...], v_ref[...]
        found = []
        for head in (0, 1):
            chosen = query * (lanes_of(head) * scale).astype(jnp.bfloat16)
            scores = contract_last(keyed, chosen) + bias_ref[...]
            top = jnp.max(scores, axis=0, keepdims=True)
            expanded = jnp.exp(scores - top)
            total = jnp.sum(expanded, axis=0, keepdims=True)
            lse_ref[head, :, :] = top + jnp.log(total)
            probs = (expanded * (1.0 / total)).astype(jnp.bfloat16)
            found.append(contract_rows(probs, valued))
        lane = lax.broadcasted_iota(jnp.int32, (1, PAIR), 1)
        out_ref[...] = jnp.where(lane < HEAD_DIM, found[0], found[1]).astype(jnp.bfloat16)

    return pl.pallas_call(
        kernel,
        grid=(pairs,),
        out_shape=[
            jax.ShapeDtypeStruct((rows, width), jnp.bfloat16),
            jax.ShapeDtypeStruct((2 * pairs, 1, rows), jnp.float32),
        ],
        in_specs=[
            pl.BlockSpec((1, rows), lambda j: (0, 0)),
            pl.BlockSpec((rows, 1), lambda j: (0, 0)),
            pl.BlockSpec((rows, PAIR), lambda j: (0, j)),
            pl.BlockSpec((rows, PAIR), lambda j: (0, pairs + j)),
            pl.BlockSpec((rows, PAIR), lambda j: (0, 2 * pairs + j)),
        ],
        out_specs=[
            pl.BlockSpec((rows, PAIR), lambda j: (0, j)),
            pl.BlockSpec((2, 1, rows), lambda j: (j, 0, 0)),
        ],
        scratch_shapes=[pltpu.VMEM((rows, rows), jnp.float32)],
        name="attend",
    )(seg_row, seg_column, qkv, qkv, qkv)


def attend_back(qkv, d_attended, lse, seg_row, seg_column):
    rows, width = qkv.shape[0], qkv.shape[1] // 3
    pairs = width // PAIR
    scale = HEAD_DIM ** (-0.5)

    def kernel(seg_row_ref, seg_column_ref, q_ref, k_ref, v_ref, d_ref, lse_ref, out_ref, bias_ref):
        step = pl.program_id(0)

        @pl.when(step == 0)
        def _():
            fill_bias(seg_row_ref, seg_column_ref, bias_ref)

        query, keyed, valued, d_out = q_ref[...], k_ref[...], v_ref[...], d_ref[...]
        scaled = query * jnp.bfloat16(scale)
        d_query, d_key, d_value = [], [], []
        for head in (0, 1):
            lanes = lanes_of(head)
            scores = contract_last(keyed, scaled * lanes) + bias_ref[...]
            probs = jnp.exp(scores - lse_ref[head, :, :])
            d_probs = contract_last(valued, d_out * lanes)
            inner = jnp.sum(probs * d_probs, axis=0, keepdims=True)
            d_scores = (probs * (d_probs - inner)).astype(jnp.bfloat16)
            d_value.append(plain_dot(probs.astype(jnp.bfloat16), d_out))
            d_key.append(plain_dot(d_scores, scaled))
            d_query.append(contract_rows(d_scores, keyed) * scale)
        lane = lax.broadcasted_iota(jnp.int32, (1, PAIR), 1)
        for at, pair in enumerate((d_query, d_key, d_value)):
            column = pl.multiple_of(at * width + step * PAIR, PAIR)
            out_ref[:, pl.ds(column, PAIR)] = jnp.where(lane < HEAD_DIM, pair[0], pair[1]).astype(
                jnp.bfloat16
            )

    return pl.pallas_call(
        kernel,
        grid=(pairs,),
        out_shape=jax.ShapeDtypeStruct((rows, 3 * width), jnp.bfloat16),
        in_specs=[
            pl.BlockSpec((1, rows), lambda j: (0, 0)),
            pl.BlockSpec((rows, 1), lambda j: (0, 0)),
            pl.BlockSpec((rows, PAIR), lambda j: (0, j)),
            pl.BlockSpec((rows, PAIR), lambda j: (0, pairs + j)),
            pl.BlockSpec((rows, PAIR), lambda j: (0, 2 * pairs + j)),
            pl.BlockSpec((rows, PAIR), lambda j: (0, j)),
            pl.BlockSpec((2, 1, rows), lambda j: (j, 0, 0)),
        ],
        out_specs=pl.BlockSpec((rows, 3 * width), lambda j: (0, 0)),
        scratch_shapes=[pltpu.VMEM((rows, rows), jnp.float32)],
        name="attend_back",
    )(seg_row, seg_column, qkv, qkv, qkv, d_attended, lse)


def swap_cores(values):
    return lax.ppermute(values, "core", [(0, 1), (1, 0)])


def reduce_near(parts):
    kept = jnp.stack([part[0] for part in parts])
    got = swap_cores(jnp.stack([part[1] for part in parts]))
    total = (kept.astype(jnp.float32) + got.astype(jnp.float32)).astype(jnp.bfloat16)
    total = total.reshape(-1, total.shape[-1])
    return lax.psum_scatter(total, SAME_CORE, scatter_dimension=0, tiled=True).astype(jnp.float32)


def relative_order(values, near_only):
    width = values.shape[1]
    chips = lax.axis_size("chips")
    chip, core = lax.axis_index("chips"), lax.axis_index("core")
    share = width // (2 * chips)
    column = lax.broadcasted_iota(jnp.int32, (width, width), 1)
    row = lax.broadcasted_iota(jnp.int32, (width, width), 0)
    core_at = (column // (width // 2)) ^ core
    if near_only:
        chip_at = (column // share) % chips
    else:
        cross_at = (column // (width // 4)) % 2
        line_at = (column // share) % (chips // 2)
        chip_at = (line_at * 2 + cross_at) ^ chip
    wanted = (chip_at * 2 + core_at) * share + column % share
    return plain_dot(values, (row == wanted).astype(jnp.bfloat16)).astype(jnp.bfloat16)


def swap_sides(values):
    return lax.ppermute(values, "tensor", [(0, 1), (1, 0)])


def swap_chips(values, bit):
    return lax.ppermute(values, "chips", [(i, i ^ bit) for i in range(lax.axis_size("chips"))])


def add_low(left, right):
    return (left.astype(jnp.float32) + right.astype(jnp.float32)).astype(jnp.bfloat16)


def halve_line(values):
    bit = lax.axis_size("chips") // 2
    while bit > 1:
        half = values.shape[0] // 2
        got = swap_chips(values[half:], bit)
        values = values[:half].astype(jnp.float32) + got.astype(jnp.float32)
        bit //= 2
        if bit > 1:
            values = values.astype(jnp.bfloat16)
    return values


def place(whole, rows, index):
    tokens, width = whole.shape
    count = rows.shape[0]
    step = 512

    def kernel(index_ref, whole_ref, rows_ref, out_ref):
        at = pl.program_id(0) * step + lax.broadcasted_iota(jnp.int32, (step, count), 0)
        hit = (at == index_ref[...]).astype(jnp.float32)
        routed = jnp.sum(hit, axis=1, keepdims=True) > 0.5
        found = plain_dot(hit.astype(jnp.bfloat16), rows_ref[...])
        out_ref[...] = jnp.where(routed, found, whole_ref[...].astype(jnp.float32)).astype(jnp.bfloat16)

    return pl.pallas_call(
        kernel,
        grid=(tokens // step,),
        out_shape=jax.ShapeDtypeStruct(whole.shape, whole.dtype),
        in_specs=[
            pl.BlockSpec((1, count), lambda i: (0, 0)),
            pl.BlockSpec((step, width), lambda i: (i, 0)),
            pl.BlockSpec((count, width), lambda i: (0, 0)),
        ],
        out_specs=pl.BlockSpec((step, width), lambda i: (i, 0)),
        name="place_rows",
    )(index[None, :], whole, rows)


def sum_everywhere(values):
    values = values + swap_cores(values)
    values = values + swap_sides(values)
    count, bit = lax.axis_size("chips"), 1
    while bit < count:
        values = values + swap_chips(values, bit)
        bit *= 2
    return values


def block(
    block_input,
    output_cot,
    segment_ids,
    routed_index,
    w_query,
    w_key,
    w_value,
    w_output,
    w_up,
    w_down,
    attn_gain,
    mlp_gain,
    router_w,
):
    side = lax.axis_index("tensor")
    sides = lax.axis_size("tensor")
    rank = lax.axis_index(DP)
    width = block_input.shape[1]
    share, heads = w_query.shape
    hidden = w_up.shape[1]

    vectors = jnp.stack([attn_gain, mlp_gain, router_w], axis=1)
    vectors = jnp.pad(vectors, ((0, 0), (0, 128 - 3)))
    near = jnp.concatenate([w_query, w_key, w_value, w_output, vectors], axis=1)
    near = lax.all_gather(near, ALL, axis=0, tiled=True).reshape(sides, width, -1)
    far = jnp.concatenate([w_up, w_down], axis=1)
    far = lax.all_gather(far, ALL, axis=0, tiled=True).reshape(sides, width, -1)
    full_qkv = [near[t, :, : 3 * heads] for t in range(sides)]
    full_output = [near[t, :, 3 * heads : 4 * heads] for t in range(sides)]
    full_up = [far[t, :, :hidden] for t in range(sides)]
    full_down = [far[t, :, hidden:] for t in range(sides)]
    small = near[0, :, 4 * heads : 4 * heads + 3].astype(jnp.float32).T
    attn_gain_f, mlp_gain_f, router_f = small[0], small[1], small[2]

    own_index = lax.dynamic_index_in_dim(routed_index, side, 0, keepdims=False)
    own_segments = lax.dynamic_index_in_dim(segment_ids, side, 0, keepdims=False)
    input_float = jnp.take(block_input, own_index, axis=0).astype(jnp.float32)
    cot_rows = jnp.take(output_cot, own_index, axis=0).astype(jnp.float32)
    firsts = jnp.sum(
        (own_segments[None, :] < jnp.arange(1, DOCS, dtype=jnp.int32)[:, None]).astype(jnp.int32), axis=1
    )
    seg_routed = jnp.sum((own_index[:, None] >= firsts[None, :]).astype(jnp.int32), axis=1)
    seg_row, seg_column = seg_routed[None, :], seg_routed[:, None]

    normed_attn = rms_norm(input_float, attn_gain_f).astype(jnp.bfloat16)
    gate = jax.nn.sigmoid(jnp.sum(input_float * router_f, axis=-1))
    d_branch = gate[:, None] * cot_rows
    d_mlp_low = d_branch.astype(jnp.bfloat16)

    qkv = [plain_dot(normed_attn, full_qkv[t]).astype(jnp.bfloat16) for t in range(sides)]
    attended, lse = zip(*[attend(qkv[t], seg_row, seg_column) for t in range(sides)])
    branch_attn = sum(contract_last(attended[t], full_output[t]) for t in range(sides))
    middle = input_float + branch_attn
    normed_mlp = rms_norm(middle, mlp_gain_f).astype(jnp.bfloat16)

    hidden_pre = [plain_dot(normed_mlp, full_up[t]) for t in range(sides)]
    hidden_act = [jax.nn.gelu(hidden_pre[t], approximate=True).astype(jnp.bfloat16) for t in range(sides)]
    d_pre = []
    for t in range(sides):
        _, gelu_back = jax.vjp(partial(jax.nn.gelu, approximate=True), hidden_pre[t])
        d_pre.append(gelu_back(plain_dot(d_mlp_low, full_down[t]))[0].astype(jnp.bfloat16))
    own_pre = [jnp.where(side == 0, d_pre[t], d_pre[1 - t]) for t in range(sides)]
    own_act = [jnp.where(side == 0, hidden_act[t], hidden_act[1 - t]) for t in range(sides)]
    left_up = relative_order(normed_mlp, False)
    left_down = relative_order(d_mlp_low, False)
    half = width // 2
    sent_up = [contract_rows(left_up[:, half:], own_pre[t]).astype(jnp.bfloat16) for t in (1, 0)][::-1]
    sent_down = [contract_rows(left_down[:, half:], own_act[t]).astype(jnp.bfloat16) for t in (1, 0)][::-1]
    got_up = [swap_cores(sent_up[t]) for t in (1, 0)][::-1]
    got_down = [swap_cores(sent_down[t]) for t in (1, 0)][::-1]
    d_pre, sent_up, sent_down = lax.optimization_barrier((d_pre, sent_up, sent_down))
    part_up = [add_low(contract_rows(left_up[:, :half], own_pre[t]), got_up[t]) for t in (0, 1)]
    part_down = [add_low(contract_rows(left_down[:, :half], own_act[t]), got_down[t]) for t in (0, 1)]
    quarter = half // 2
    got_up = swap_sides(part_up[1])
    got_down = [swap_chips(part_down[t][quarter:], 1) for t in (0, 1)]
    one_up = add_low(part_up[0], got_up)
    one_down = [add_low(part_down[t][:quarter], got_down[t]) for t in (0, 1)]
    got_up = swap_chips(one_up[quarter:], 1)
    got_down = swap_sides(one_down[1])
    sum_up = halve_line(add_low(one_up[:quarter], got_up))
    sum_down = halve_line(add_low(one_down[0], got_down))

    d_normed_mlp = sum(contract_last(d_pre[t], full_up[t]) for t in range(sides))
    _, norm_back_mlp = jax.vjp(rms_norm, middle, mlp_gain_f)
    d_middle, d_mlp_gain = norm_back_mlp(d_normed_mlp)
    d_attn_low = (d_branch + d_middle).astype(jnp.bfloat16)
    d_qkv = []
    for t in range(sides):
        d_attended = plain_dot(d_attn_low, full_output[t]).astype(jnp.bfloat16)
        d_qkv.append(attend_back(qkv[t], d_attended, lse[t], seg_row, seg_column))
    left_qkv = relative_order(normed_attn, True)
    left_output = relative_order(d_attn_low, True)
    grad_attn = [
        [
            jnp.concatenate(
                [
                    contract_rows(left_qkv[:, rows], d_qkv[t]),
                    contract_rows(left_output[:, rows], attended[t]),
                ],
                axis=1,
            ).astype(jnp.bfloat16)
            for rows in (slice(0, half), slice(half, width))
        ]
        for t in range(sides)
    ]
    sum_attn = reduce_near(grad_attn)

    branch_mlp = sum(contract_last(hidden_act[t], full_down[t]) for t in range(sides))
    branch_total = branch_attn + branch_mlp
    updated = input_float + gate[:, None] * branch_total
    block_output = place(block_input, updated.astype(jnp.bfloat16), own_index)
    d_logit = gate * (1.0 - gate) * jnp.sum(cot_rows * branch_total, axis=-1)

    d_normed_attn = sum(contract_last(d_qkv[t], full_qkv[t]) for t in range(sides))
    _, norm_back_attn = jax.vjp(rms_norm, input_float, attn_gain_f)
    d_input_norm, d_attn_gain = norm_back_attn(d_normed_attn)
    d_router = jnp.sum(d_logit[:, None] * input_float, axis=0)
    routed_grad = cot_rows + d_logit[:, None] * router_f + d_middle + d_input_norm
    block_grad = place(output_cot, routed_grad.astype(jnp.bfloat16), own_index)

    totals = sum_everywhere(jnp.stack([d_attn_gain, d_mlp_gain, d_router]))
    own = lax.dynamic_slice_in_dim(totals, rank * share, share, axis=1)
    return (
        block_output,
        block_grad,
        sum_attn[:, :heads],
        sum_attn[:, heads : 2 * heads],
        sum_attn[:, 2 * heads : 3 * heads],
        sum_attn[:, 3 * heads :],
        sum_up,
        sum_down,
        own[0],
        own[1],
        own[2],
    )


def solution(mesh):
    fine = Mesh(mesh.devices.reshape(-1, 2, mesh.shape["tensor"]), ("chips", "core", "tensor"))
    token = P(("chips", "core", "tensor"), None)
    weight = P(DP, "tensor")
    in_specs = (token, token, P(DP, None), P(DP, None)) + (weight,) * 6 + (P(DP),) * 3
    out_specs = (token, token) + (weight,) * 6 + (P(DP),) * 3
    return jax.shard_map(block, mesh=fine, in_specs=in_specs, out_specs=out_specs, check_vma=False)
```

```python
from functools import partial

import jax
import jax.numpy as jnp
from jax import lax
from jax.experimental import pallas as pl
from jax.experimental.pallas import tpu as pltpu
from jax.sharding import Mesh
from jax.sharding import PartitionSpec as P


HEAD_DIM = 64
EPSILON = 1e-05
DOCS = 16
PAIR = 2 * HEAD_DIM
DP = ("chips", "core")
ALL = ("tensor", "chips", "core")
SAME_CORE = ("tensor", "chips")


def rms_norm(values, gain):
    scale = lax.rsqrt(jnp.mean(values * values, axis=-1, keepdims=True) + EPSILON)
    return values * scale * gain


def plain_dot(left, right):
    return jnp.dot(left, right, preferred_element_type=jnp.float32)


def contract_rows(left, right):
    return lax.dot_general(
        left, right, (((0,), (0,)), ((), ())), preferred_element_type=jnp.float32
    )


def contract_last(left, right):
    return lax.dot_general(
        left, right, (((1,), (1,)), ((), ())), preferred_element_type=jnp.float32
    )


def fill_bias(seg_row_ref, seg_column_ref, bias_ref):
    rows = bias_ref.shape[0]
    key_at = lax.broadcasted_iota(jnp.int32, (rows, rows), 0)
    query_at = lax.broadcasted_iota(jnp.int32, (rows, rows), 1)
    same = seg_column_ref[...] == seg_row_ref[...]
    bias_ref[...] = jnp.where(same & (key_at <= query_at), 0.0, -1e30)


def lanes_of(head):
    lane = lax.broadcasted_iota(jnp.int32, (1, PAIR), 1)
    return (lane // HEAD_DIM == head).astype(jnp.bfloat16)


def attend(qkv, seg_row, seg_column):
    rows, width = qkv.shape[0], qkv.shape[1] // 3
    pairs = width // PAIR
    scale = HEAD_DIM ** (-0.5)

    def kernel(seg_row_ref, seg_column_ref, q_ref, k_ref, v_ref, out_ref, lse_ref, bias_ref):
        @pl.when(pl.program_id(0) == 0)
        def _():
            fill_bias(seg_row_ref, seg_column_ref, bias_ref)

        query, keyed, valued = q_ref[...], k_ref[...], v_ref[...]
        found = []
        for head in (0, 1):
            chosen = query * (lanes_of(head) * scale).astype(jnp.bfloat16)
            scores = contract_last(keyed, chosen) + bias_ref[...]
            top = jnp.max(scores, axis=0, keepdims=True)
            expanded = jnp.exp(scores - top)
            total = jnp.sum(expanded, axis=0, keepdims=True)
            lse_ref[head, :, :] = top + jnp.log(total)
            probs = (expanded * (1.0 / total)).astype(jnp.bfloat16)
            found.append(contract_rows(probs, valued))
        lane = lax.broadcasted_iota(jnp.int32, (1, PAIR), 1)
        out_ref[...] = jnp.where(lane < HEAD_DIM, found[0], found[1]).astype(jnp.bfloat16)

    return pl.pallas_call(
        kernel,
        grid=(pairs,),
        out_shape=[
            jax.ShapeDtypeStruct((rows, width), jnp.bfloat16),
            jax.ShapeDtypeStruct((2 * pairs, 1, rows), jnp.float32),
        ],
        in_specs=[
            pl.BlockSpec((1, rows), lambda j: (0, 0)),
            pl.BlockSpec((rows, 1), lambda j: (0, 0)),
            pl.BlockSpec((rows, PAIR), lambda j: (0, j)),
            pl.BlockSpec((rows, PAIR), lambda j: (0, pairs + j)),
            pl.BlockSpec((rows, PAIR), lambda j: (0, 2 * pairs + j)),
        ],
        out_specs=[
            pl.BlockSpec((rows, PAIR), lambda j: (0, j)),
            pl.BlockSpec((2, 1, rows), lambda j: (j, 0, 0)),
        ],
        scratch_shapes=[pltpu.VMEM((rows, rows), jnp.float32)],
        name="attend",
    )(seg_row, seg_column, qkv, qkv, qkv)


def attend_back(qkv, d_attended, lse, seg_row, seg_column):
    rows, width = qkv.shape[0], qkv.shape[1] // 3
    pairs = width // PAIR
    scale = HEAD_DIM ** (-0.5)

    def kernel(seg_row_ref, seg_column_ref, q_ref, k_ref, v_ref, d_ref, lse_ref, out_ref, bias_ref):
        step = pl.program_id(0)

        @pl.when(step == 0)
        def _():
            fill_bias(seg_row_ref, seg_column_ref, bias_ref)

        query, keyed, valued, d_out = q_ref[...], k_ref[...], v_ref[...], d_ref[...]
        scaled = query * jnp.bfloat16(scale)
        d_query, d_key, d_value = [], [], []
        for head in (0, 1):
            lanes = lanes_of(head)
            scores = contract_last(keyed, scaled * lanes) + bias_ref[...]
            probs = jnp.exp(scores - lse_ref[head, :, :])
            d_probs = contract_last(valued, d_out * lanes)
            inner = jnp.sum(probs * d_probs, axis=0, keepdims=True)
            d_scores = (probs * (d_probs - inner)).astype(jnp.bfloat16)
            d_value.append(plain_dot(probs.astype(jnp.bfloat16), d_out))
            d_key.append(plain_dot(d_scores, scaled))
            d_query.append(contract_rows(d_scores, keyed) * scale)
        lane = lax.broadcasted_iota(jnp.int32, (1, PAIR), 1)
        for at, pair in enumerate((d_query, d_key, d_value)):
            column = pl.multiple_of(at * width + step * PAIR, PAIR)
            out_ref[:, pl.ds(column, PAIR)] = jnp.where(lane < HEAD_DIM, pair[0], pair[1]).astype(
                jnp.bfloat16
            )

    return pl.pallas_call(
        kernel,
        grid=(pairs,),
        out_shape=jax.ShapeDtypeStruct((rows, 3 * width), jnp.bfloat16),
        in_specs=[
            pl.BlockSpec((1, rows), lambda j: (0, 0)),
            pl.BlockSpec((rows, 1), lambda j: (0, 0)),
            pl.BlockSpec((rows, PAIR), lambda j: (0, j)),
            pl.BlockSpec((rows, PAIR), lambda j: (0, pairs + j)),
            pl.BlockSpec((rows, PAIR), lambda j: (0, 2 * pairs + j)),
            pl.BlockSpec((rows, PAIR), lambda j: (0, j)),
            pl.BlockSpec((2, 1, rows), lambda j: (j, 0, 0)),
        ],
        out_specs=pl.BlockSpec((rows, 3 * width), lambda j: (0, 0)),
        scratch_shapes=[pltpu.VMEM((rows, rows), jnp.float32)],
        name="attend_back",
    )(seg_row, seg_column, qkv, qkv, qkv, d_attended, lse)


def swap_cores(values):
    return lax.ppermute(values, "core", [(0, 1), (1, 0)])


def reduce_near(parts):
    kept = jnp.stack([part[0] for part in parts])
    got = swap_cores(jnp.stack([part[1] for part in parts]))
    total = (kept.astype(jnp.float32) + got.astype(jnp.float32)).astype(jnp.bfloat16)
    total = total.reshape(-1, total.shape[-1])
    return lax.psum_scatter(total, SAME_CORE, scatter_dimension=0, tiled=True).astype(jnp.float32)


def relative_order(values, near_only):
    width = values.shape[1]
    chips = lax.axis_size("chips")
    chip, core = lax.axis_index("chips"), lax.axis_index("core")
    share = width // (2 * chips)
    column = lax.broadcasted_iota(jnp.int32, (width, width), 1)
    row = lax.broadcasted_iota(jnp.int32, (width, width), 0)
    core_at = (column // (width // 2)) ^ core
    if near_only:
        chip_at = (column // share) % chips
    else:
        cross_at = (column // (width // 4)) % 2
        line_at = (column // share) % (chips // 2)
        chip_at = (line_at * 2 + cross_at) ^ chip
    wanted = (chip_at * 2 + core_at) * share + column % share
    return plain_dot(values, (row == wanted).astype(jnp.bfloat16)).astype(jnp.bfloat16)


def swap_sides(values):
    return lax.ppermute(values, "tensor", [(0, 1), (1, 0)])


def swap_chips(values, bit):
    return lax.ppermute(values, "chips", [(i, i ^ bit) for i in range(lax.axis_size("chips"))])


def add_low(left, right):
    return (left.astype(jnp.float32) + right.astype(jnp.float32)).astype(jnp.bfloat16)


def halve_line(values):
    bit = lax.axis_size("chips") // 2
    while bit > 1:
        half = values.shape[0] // 2
        got = swap_chips(values[half:], bit)
        values = values[:half].astype(jnp.float32) + got.astype(jnp.float32)
        bit //= 2
        if bit > 1:
            values = values.astype(jnp.bfloat16)
    return values


def place(whole, rows, index):
    tokens, width = whole.shape
    count = rows.shape[0]
    step = 512

    def kernel(index_ref, whole_ref, rows_ref, out_ref):
        at = pl.program_id(0) * step + lax.broadcasted_iota(jnp.int32, (step, count), 0)
        hit = (at == index_ref[...]).astype(jnp.float32)
        routed = jnp.sum(hit, axis=1, keepdims=True) > 0.5
        found = plain_dot(hit.astype(jnp.bfloat16), rows_ref[...])
        out_ref[...] = jnp.where(routed, found, whole_ref[...].astype(jnp.float32)).astype(jnp.bfloat16)

    return pl.pallas_call(
        kernel,
        grid=(tokens // step,),
        out_shape=jax.ShapeDtypeStruct(whole.shape, whole.dtype),
        in_specs=[
            pl.BlockSpec((1, count), lambda i: (0, 0)),
            pl.BlockSpec((step, width), lambda i: (i, 0)),
            pl.BlockSpec((count, width), lambda i: (0, 0)),
        ],
        out_specs=pl.BlockSpec((step, width), lambda i: (i, 0)),
        name="place_rows",
    )(index[None, :], whole, rows)


def sum_everywhere(values):
    values = values + swap_cores(values)
    values = values + swap_chips(values, 1)
    values = values + swap_sides(values)
    bit = lax.axis_size("chips") // 2
    while bit > 1:
        values = values + swap_chips(values, bit)
        bit //= 2
    return values


def block(
    block_input,
    output_cot,
    segment_ids,
    routed_index,
    w_query,
    w_key,
    w_value,
    w_output,
    w_up,
    w_down,
    attn_gain,
    mlp_gain,
    router_w,
):
    side = lax.axis_index("tensor")
    sides = lax.axis_size("tensor")
    rank = lax.axis_index(DP)
    width = block_input.shape[1]
    share, heads = w_query.shape
    hidden = w_up.shape[1]

    vectors = jnp.stack([attn_gain, mlp_gain, router_w], axis=1)
    vectors = jnp.pad(vectors, ((0, 0), (0, 128 - 3)))
    near = jnp.concatenate([w_query, w_key, w_value, w_output, vectors], axis=1)
    near = lax.all_gather(near, ALL, axis=0, tiled=True).reshape(sides, width, -1)
    far = jnp.concatenate([w_up, w_down], axis=1)
    far = lax.all_gather(far, ALL, axis=0, tiled=True).reshape(sides, width, -1)
    full_qkv = [near[t, :, : 3 * heads] for t in range(sides)]
    full_output = [near[t, :, 3 * heads : 4 * heads] for t in range(sides)]
    full_up = [far[t, :, :hidden] for t in range(sides)]
    full_down = [far[t, :, hidden:] for t in range(sides)]
    small = near[0, :, 4 * heads : 4 * heads + 3].astype(jnp.float32).T
    attn_gain_f, mlp_gain_f, router_f = small[0], small[1], small[2]

    own_index = lax.dynamic_index_in_dim(routed_index, side, 0, keepdims=False)
    own_segments = lax.dynamic_index_in_dim(segment_ids, side, 0, keepdims=False)
    input_float = jnp.take(block_input, own_index, axis=0).astype(jnp.float32)
    cot_rows = jnp.take(output_cot, own_index, axis=0).astype(jnp.float32)
    firsts = jnp.sum(
        (own_segments[None, :] < jnp.arange(1, DOCS, dtype=jnp.int32)[:, None]).astype(jnp.int32), axis=1
    )
    seg_routed = jnp.sum((own_index[:, None] >= firsts[None, :]).astype(jnp.int32), axis=1)
    seg_row, seg_column = seg_routed[None, :], seg_routed[:, None]

    normed_attn = rms_norm(input_float, attn_gain_f).astype(jnp.bfloat16)
    gate = jax.nn.sigmoid(jnp.sum(input_float * router_f, axis=-1))
    d_branch = gate[:, None] * cot_rows
    d_mlp_low = d_branch.astype(jnp.bfloat16)

    qkv = [plain_dot(normed_attn, full_qkv[t]).astype(jnp.bfloat16) for t in range(sides)]
    attended, lse = zip(*[attend(qkv[t], seg_row, seg_column) for t in range(sides)])
    branch_attn = sum(contract_last(attended[t], full_output[t]) for t in range(sides))
    middle = input_float + branch_attn
    normed_mlp = rms_norm(middle, mlp_gain_f).astype(jnp.bfloat16)

    hidden_pre = [plain_dot(normed_mlp, full_up[t]) for t in range(sides)]
    hidden_act = [jax.nn.gelu(hidden_pre[t], approximate=True).astype(jnp.bfloat16) for t in range(sides)]
    d_pre = []
    for t in range(sides):
        _, gelu_back = jax.vjp(partial(jax.nn.gelu, approximate=True), hidden_pre[t])
        d_pre.append(gelu_back(plain_dot(d_mlp_low, full_down[t]))[0].astype(jnp.bfloat16))
    own_pre = [jnp.where(side == 0, d_pre[t], d_pre[1 - t]) for t in range(sides)]
    own_act = [jnp.where(side == 0, hidden_act[t], hidden_act[1 - t]) for t in range(sides)]
    left_up = relative_order(normed_mlp, False)
    left_down = relative_order(d_mlp_low, False)
    half = width // 2
    sent_up = [contract_rows(left_up[:, half:], own_pre[t]).astype(jnp.bfloat16) for t in (1, 0)][::-1]
    sent_down = [contract_rows(left_down[:, half:], own_act[t]).astype(jnp.bfloat16) for t in (1, 0)][::-1]
    got_up = [swap_cores(sent_up[t]) for t in (1, 0)][::-1]
    got_down = [swap_cores(sent_down[t]) for t in (1, 0)][::-1]
    d_pre, sent_up, sent_down = lax.optimization_barrier((d_pre, sent_up, sent_down))
    part_up = [add_low(contract_rows(left_up[:, :half], own_pre[t]), got_up[t]) for t in (0, 1)]
    part_down = [add_low(contract_rows(left_down[:, :half], own_act[t]), got_down[t]) for t in (0, 1)]
    quarter = half // 2
    got_up = swap_sides(part_up[1])
    got_down = [swap_chips(part_down[t][quarter:], 1) for t in (0, 1)]
    one_up = add_low(part_up[0], got_up)
    one_down = [add_low(part_down[t][:quarter], got_down[t]) for t in (0, 1)]
    got_up = swap_chips(one_up[quarter:], 1)
    got_down = swap_sides(one_down[1])
    sum_up = halve_line(add_low(one_up[:quarter], got_up))
    sum_down = halve_line(add_low(one_down[0], got_down))

    d_normed_mlp = sum(contract_last(d_pre[t], full_up[t]) for t in range(sides))
    _, norm_back_mlp = jax.vjp(rms_norm, middle, mlp_gain_f)
    d_middle, d_mlp_gain = norm_back_mlp(d_normed_mlp)
    d_attn_low = (d_branch + d_middle).astype(jnp.bfloat16)
    d_qkv = []
    for t in range(sides):
        d_attended = plain_dot(d_attn_low, full_output[t]).astype(jnp.bfloat16)
        d_qkv.append(attend_back(qkv[t], d_attended, lse[t], seg_row, seg_column))
    left_qkv = relative_order(normed_attn, True)
    left_output = relative_order(d_attn_low, True)
    grad_attn = [
        [
            jnp.concatenate(
                [
                    contract_rows(left_qkv[:, rows], d_qkv[t]),
                    contract_rows(left_output[:, rows], attended[t]),
                ],
                axis=1,
            ).astype(jnp.bfloat16)
            for rows in (slice(0, half), slice(half, width))
        ]
        for t in range(sides)
    ]
    sum_attn = reduce_near(grad_attn)

    d_qkv, hidden_act = lax.optimization_barrier((d_qkv, hidden_act))
    branch_mlp = sum(contract_last(hidden_act[t], full_down[t]) for t in range(sides))
    branch_total = branch_attn + branch_mlp
    updated = input_float + gate[:, None] * branch_total
    block_output = place(block_input, updated.astype(jnp.bfloat16), own_index)
    d_logit = gate * (1.0 - gate) * jnp.sum(cot_rows * branch_total, axis=-1)

    d_normed_attn = sum(contract_last(d_qkv[t], full_qkv[t]) for t in range(sides))
    _, norm_back_attn = jax.vjp(rms_norm, input_float, attn_gain_f)
    d_input_norm, d_attn_gain = norm_back_attn(d_normed_attn)
    d_router = jnp.sum(d_logit[:, None] * input_float, axis=0)
    routed_grad = cot_rows + d_logit[:, None] * router_f + d_middle + d_input_norm
    block_grad = place(output_cot, routed_grad.astype(jnp.bfloat16), own_index)

    totals = sum_everywhere(jnp.stack([d_attn_gain, d_mlp_gain, d_router]))
    own = lax.dynamic_slice_in_dim(totals, rank * share, share, axis=1)
    return (
        block_output,
        block_grad,
        sum_attn[:, :heads],
        sum_attn[:, heads : 2 * heads],
        sum_attn[:, 2 * heads : 3 * heads],
        sum_attn[:, 3 * heads :],
        sum_up,
        sum_down,
        own[0],
        own[1],
        own[2],
    )


def solution(mesh):
    fine = Mesh(mesh.devices.reshape(-1, 2, mesh.shape["tensor"]), ("chips", "core", "tensor"))
    token = P(("chips", "core", "tensor"), None)
    weight = P(DP, "tensor")
    in_specs = (token, token, P(DP, None), P(DP, None)) + (weight,) * 6 + (P(DP),) * 3
    out_specs = (token, token) + (weight,) * 6 + (P(DP),) * 3
    return jax.shard_map(block, mesh=fine, in_specs=in_specs, out_specs=out_specs, check_vma=False)
```

```python
from functools import partial

import jax
import jax.numpy as jnp
from jax import lax
from jax.experimental import pallas as pl
from jax.experimental.pallas import tpu as pltpu
from jax.sharding import Mesh
from jax.sharding import PartitionSpec as P


HEAD_DIM = 64
EPSILON = 1e-05
DOCS = 16
PAIR = 2 * HEAD_DIM
DP = ("chips", "core")
ALL = ("tensor", "chips", "core")
SAME_CORE = ("tensor", "chips")


def rms_norm(values, gain):
    scale = lax.rsqrt(jnp.mean(values * values, axis=-1, keepdims=True) + EPSILON)
    return values * scale * gain


def plain_dot(left, right):
    return jnp.dot(left, right, preferred_element_type=jnp.float32)


def contract_rows(left, right):
    return lax.dot_general(
        left, right, (((0,), (0,)), ((), ())), preferred_element_type=jnp.float32
    )


def contract_last(left, right):
    return lax.dot_general(
        left, right, (((1,), (1,)), ((), ())), preferred_element_type=jnp.float32
    )


def fill_bias(seg_row_ref, seg_column_ref, bias_ref):
    rows = bias_ref.shape[0]
    key_at = lax.broadcasted_iota(jnp.int32, (rows, rows), 0)
    query_at = lax.broadcasted_iota(jnp.int32, (rows, rows), 1)
    same = seg_column_ref[...] == seg_row_ref[...]
    bias_ref[...] = jnp.where(same & (key_at <= query_at), 0.0, -1e30)


def lanes_of(head):
    lane = lax.broadcasted_iota(jnp.int32, (1, PAIR), 1)
    return (lane // HEAD_DIM == head).astype(jnp.bfloat16)


def attend(qkv, seg_row, seg_column):
    rows, width = qkv.shape[0], qkv.shape[1] // 3
    pairs = width // PAIR
    scale = HEAD_DIM ** (-0.5)

    def kernel(seg_row_ref, seg_column_ref, q_ref, k_ref, v_ref, out_ref, lse_ref, bias_ref):
        @pl.when(pl.program_id(0) == 0)
        def _():
            fill_bias(seg_row_ref, seg_column_ref, bias_ref)

        query, keyed, valued = q_ref[...], k_ref[...], v_ref[...]
        found = []
        for head in (0, 1):
            chosen = query * (lanes_of(head) * scale).astype(jnp.bfloat16)
            scores = contract_last(keyed, chosen) + bias_ref[...]
            top = jnp.max(scores, axis=0, keepdims=True)
            expanded = jnp.exp(scores - top)
            total = jnp.sum(expanded, axis=0, keepdims=True)
            lse_ref[head, :, :] = top + jnp.log(total)
            probs = (expanded * (1.0 / total)).astype(jnp.bfloat16)
            found.append(contract_rows(probs, valued))
        lane = lax.broadcasted_iota(jnp.int32, (1, PAIR), 1)
        out_ref[...] = jnp.where(lane < HEAD_DIM, found[0], found[1]).astype(jnp.bfloat16)

    return pl.pallas_call(
        kernel,
        grid=(pairs,),
        out_shape=[
            jax.ShapeDtypeStruct((rows, width), jnp.bfloat16),
            jax.ShapeDtypeStruct((2 * pairs, 1, rows), jnp.float32),
        ],
        in_specs=[
            pl.BlockSpec((1, rows), lambda j: (0, 0)),
            pl.BlockSpec((rows, 1), lambda j: (0, 0)),
            pl.BlockSpec((rows, PAIR), lambda j: (0, j)),
            pl.BlockSpec((rows, PAIR), lambda j: (0, pairs + j)),
            pl.BlockSpec((rows, PAIR), lambda j: (0, 2 * pairs + j)),
        ],
        out_specs=[
            pl.BlockSpec((rows, PAIR), lambda j: (0, j)),
            pl.BlockSpec((2, 1, rows), lambda j: (j, 0, 0)),
        ],
        scratch_shapes=[pltpu.VMEM((rows, rows), jnp.float32)],
        name="attend",
    )(seg_row, seg_column, qkv, qkv, qkv)


def attend_back(qkv, d_attended, lse, seg_row, seg_column):
    rows, width = qkv.shape[0], qkv.shape[1] // 3
    pairs = width // PAIR
    scale = HEAD_DIM ** (-0.5)

    def kernel(seg_row_ref, seg_column_ref, q_ref, k_ref, v_ref, d_ref, lse_ref, out_ref, bias_ref):
        step = pl.program_id(0)

        @pl.when(step == 0)
        def _():
            fill_bias(seg_row_ref, seg_column_ref, bias_ref)

        query, keyed, valued, d_out = q_ref[...], k_ref[...], v_ref[...], d_ref[...]
        scaled = query * jnp.bfloat16(scale)
        d_query, d_key, d_value = [], [], []
        for head in (0, 1):
            lanes = lanes_of(head)
            scores = contract_last(keyed, scaled * lanes) + bias_ref[...]
            probs = jnp.exp(scores - lse_ref[head, :, :])
            d_probs = contract_last(valued, d_out * lanes)
            inner = jnp.sum(probs * d_probs, axis=0, keepdims=True)
            d_scores = (probs * (d_probs - inner)).astype(jnp.bfloat16)
            d_value.append(plain_dot(probs.astype(jnp.bfloat16), d_out))
            d_key.append(plain_dot(d_scores, scaled))
            d_query.append(contract_rows(d_scores, keyed) * scale)
        lane = lax.broadcasted_iota(jnp.int32, (1, PAIR), 1)
        for at, pair in enumerate((d_query, d_key, d_value)):
            column = pl.multiple_of(at * width + step * PAIR, PAIR)
            out_ref[:, pl.ds(column, PAIR)] = jnp.where(lane < HEAD_DIM, pair[0], pair[1]).astype(
                jnp.bfloat16
            )

    return pl.pallas_call(
        kernel,
        grid=(pairs,),
        out_shape=jax.ShapeDtypeStruct((rows, 3 * width), jnp.bfloat16),
        in_specs=[
            pl.BlockSpec((1, rows), lambda j: (0, 0)),
            pl.BlockSpec((rows, 1), lambda j: (0, 0)),
            pl.BlockSpec((rows, PAIR), lambda j: (0, j)),
            pl.BlockSpec((rows, PAIR), lambda j: (0, pairs + j)),
            pl.BlockSpec((rows, PAIR), lambda j: (0, 2 * pairs + j)),
            pl.BlockSpec((rows, PAIR), lambda j: (0, j)),
            pl.BlockSpec((2, 1, rows), lambda j: (j, 0, 0)),
        ],
        out_specs=pl.BlockSpec((rows, 3 * width), lambda j: (0, 0)),
        scratch_shapes=[pltpu.VMEM((rows, rows), jnp.float32)],
        name="attend_back",
    )(seg_row, seg_column, qkv, qkv, qkv, d_attended, lse)


def swap_cores(values):
    return lax.ppermute(values, "core", [(0, 1), (1, 0)])


def reduce_near(parts):
    kept = jnp.stack([part[0] for part in parts])
    got = swap_cores(jnp.stack([part[1] for part in parts]))
    total = (kept.astype(jnp.float32) + got.astype(jnp.float32)).astype(jnp.bfloat16)
    total = total.reshape(-1, total.shape[-1])
    return lax.psum_scatter(total, SAME_CORE, scatter_dimension=0, tiled=True).astype(jnp.float32)


def relative_order(values, near_only):
    width = values.shape[1]
    chips = lax.axis_size("chips")
    chip, core = lax.axis_index("chips"), lax.axis_index("core")
    share = width // (2 * chips)
    column = lax.broadcasted_iota(jnp.int32, (width, width), 1)
    row = lax.broadcasted_iota(jnp.int32, (width, width), 0)
    core_at = (column // (width // 2)) ^ core
    if near_only:
        chip_at = (column // share) % chips
    else:
        cross_at = (column // (width // 4)) % 2
        line_at = (column // share) % (chips // 2)
        chip_at = (line_at * 2 + cross_at) ^ chip
    wanted = (chip_at * 2 + core_at) * share + column % share
    return plain_dot(values, (row == wanted).astype(jnp.bfloat16)).astype(jnp.bfloat16)


def swap_sides(values):
    return lax.ppermute(values, "tensor", [(0, 1), (1, 0)])


def swap_chips(values, bit):
    return lax.ppermute(values, "chips", [(i, i ^ bit) for i in range(lax.axis_size("chips"))])


def add_low(left, right):
    return (left.astype(jnp.float32) + right.astype(jnp.float32)).astype(jnp.bfloat16)


def halve_line(values):
    bit = lax.axis_size("chips") // 2
    while bit > 1:
        half = values.shape[0] // 2
        got = swap_chips(values[half:], bit)
        values = values[:half].astype(jnp.float32) + got.astype(jnp.float32)
        bit //= 2
        if bit > 1:
            values = values.astype(jnp.bfloat16)
    return values


def halve_grads(left, right):
    half, columns = left.shape[1] // 2, right[0].shape[1]
    quarter = half // 2
    colors = (slice(0, columns // 2), slice(columns // 2, columns))
    sent = [contract_rows(left[:, half:], right[t]).astype(jnp.bfloat16) for t in (0, 1)]
    got = [swap_cores(sent[t]) for t in (0, 1)]
    part_a, part_b = [
        [add_low(contract_rows(left[:, :half], right[t][:, color]), got[t][:, color]) for t in (0, 1)]
        for color in colors
    ]
    got_a = swap_sides(part_a[1])
    got_b = [swap_chips(part_b[t][quarter:], 1) for t in (0, 1)]
    part_a = add_low(part_a[0], got_a)
    part_b = [add_low(part_b[t][:quarter], got_b[t]) for t in (0, 1)]
    got_a = swap_chips(part_a[quarter:], 1)
    got_b = swap_sides(part_b[1])
    part_a = add_low(part_a[:quarter], got_a)
    part_b = add_low(part_b[0], got_b)
    return halve_line(jnp.concatenate([part_a, part_b], axis=1)), sent


def place(whole, rows, index):
    tokens, width = whole.shape
    count = rows.shape[0]
    step = 512

    def kernel(index_ref, whole_ref, rows_ref, out_ref):
        at = pl.program_id(0) * step + lax.broadcasted_iota(jnp.int32, (step, count), 0)
        hit = (at == index_ref[...]).astype(jnp.float32)
        routed = jnp.sum(hit, axis=1, keepdims=True) > 0.5
        found = plain_dot(hit.astype(jnp.bfloat16), rows_ref[...])
        out_ref[...] = jnp.where(routed, found, whole_ref[...].astype(jnp.float32)).astype(jnp.bfloat16)

    return pl.pallas_call(
        kernel,
        grid=(tokens // step,),
        out_shape=jax.ShapeDtypeStruct(whole.shape, whole.dtype),
        in_specs=[
            pl.BlockSpec((1, count), lambda i: (0, 0)),
            pl.BlockSpec((step, width), lambda i: (i, 0)),
            pl.BlockSpec((count, width), lambda i: (0, 0)),
        ],
        out_specs=pl.BlockSpec((step, width), lambda i: (i, 0)),
        name="place_rows",
    )(index[None, :], whole, rows)


def sum_everywhere(values):
    values = values + swap_cores(values)
    values = values + swap_chips(values, 1)
    values = values + swap_sides(values)
    bit = lax.axis_size("chips") // 2
    while bit > 1:
        values = values + swap_chips(values, bit)
        bit //= 2
    return values


def block(
    block_input,
    output_cot,
    segment_ids,
    routed_index,
    w_query,
    w_key,
    w_value,
    w_output,
    w_up,
    w_down,
    attn_gain,
    mlp_gain,
    router_w,
):
    side = lax.axis_index("tensor")
    sides = lax.axis_size("tensor")
    rank = lax.axis_index(DP)
    width = block_input.shape[1]
    share, heads = w_query.shape
    hidden = w_up.shape[1]

    vectors = jnp.stack([attn_gain, mlp_gain, router_w], axis=1)
    vectors = jnp.pad(vectors, ((0, 0), (0, 128 - 3)))
    near = jnp.concatenate([w_query, w_key, w_value, w_output, w_up, vectors], axis=1)
    near = lax.all_gather(near, ALL, axis=0, tiled=True).reshape(sides, width, -1)
    far = lax.all_gather(w_down, ALL, axis=0, tiled=True).reshape(sides, width, -1)
    full_qkv = [near[t, :, : 3 * heads] for t in range(sides)]
    full_output = [near[t, :, 3 * heads : 4 * heads] for t in range(sides)]
    full_up = [near[t, :, 4 * heads : 4 * heads + hidden] for t in range(sides)]
    full_down = [far[t] for t in range(sides)]
    small = near[0, :, 4 * heads + hidden : 4 * heads + hidden + 3].astype(jnp.float32).T
    attn_gain_f, mlp_gain_f, router_f = small[0], small[1], small[2]

    own_index = lax.dynamic_index_in_dim(routed_index, side, 0, keepdims=False)
    own_segments = lax.dynamic_index_in_dim(segment_ids, side, 0, keepdims=False)
    input_float = jnp.take(block_input, own_index, axis=0).astype(jnp.float32)
    cot_rows = jnp.take(output_cot, own_index, axis=0).astype(jnp.float32)
    firsts = jnp.sum(
        (own_segments[None, :] < jnp.arange(1, DOCS, dtype=jnp.int32)[:, None]).astype(jnp.int32), axis=1
    )
    seg_routed = jnp.sum((own_index[:, None] >= firsts[None, :]).astype(jnp.int32), axis=1)
    seg_row, seg_column = seg_routed[None, :], seg_routed[:, None]

    normed_attn = rms_norm(input_float, attn_gain_f).astype(jnp.bfloat16)
    gate = jax.nn.sigmoid(jnp.sum(input_float * router_f, axis=-1))
    d_branch = gate[:, None] * cot_rows
    d_mlp_low = d_branch.astype(jnp.bfloat16)

    qkv = [plain_dot(normed_attn, full_qkv[t]).astype(jnp.bfloat16) for t in range(sides)]
    attended, lse = zip(*[attend(qkv[t], seg_row, seg_column) for t in range(sides)])
    branch_attn = sum(contract_last(attended[t], full_output[t]) for t in range(sides))
    middle = input_float + branch_attn
    normed_mlp = rms_norm(middle, mlp_gain_f).astype(jnp.bfloat16)

    hidden_pre = [plain_dot(normed_mlp, full_up[t]) for t in range(sides)]
    hidden_act = [jax.nn.gelu(hidden_pre[t], approximate=True).astype(jnp.bfloat16) for t in range(sides)]
    own_act = [jnp.where(side == 0, hidden_act[t], hidden_act[1 - t]) for t in range(sides)]
    left_down = relative_order(d_mlp_low, False)
    sum_down, _ = halve_grads(left_down, own_act)
    d_pre = []
    for t in range(sides):
        _, gelu_back = jax.vjp(partial(jax.nn.gelu, approximate=True), hidden_pre[t])
        d_act = plain_dot(d_mlp_low, full_down[t])
        d_pre.append(gelu_back(d_act)[0].astype(jnp.bfloat16))
    own_pre = [jnp.where(side == 0, d_pre[t], d_pre[1 - t]) for t in range(sides)]
    left_up = relative_order(normed_mlp, False)
    sum_up, sent_up = halve_grads(left_up, own_pre)
    d_pre, sent_up = lax.optimization_barrier((d_pre, sent_up))

    d_normed_mlp = sum(contract_last(d_pre[t], full_up[t]) for t in range(sides))
    _, norm_back_mlp = jax.vjp(rms_norm, middle, mlp_gain_f)
    d_middle, d_mlp_gain = norm_back_mlp(d_normed_mlp)
    d_attn_low = (d_branch + d_middle).astype(jnp.bfloat16)
    d_qkv = []
    for t in range(sides):
        d_attended = plain_dot(d_attn_low, full_output[t]).astype(jnp.bfloat16)
        d_qkv.append(attend_back(qkv[t], d_attended, lse[t], seg_row, seg_column))
    half = width // 2
    left_qkv = relative_order(normed_attn, True)
    left_output = relative_order(d_attn_low, True)
    grad_attn = [
        [
            jnp.concatenate(
                [
                    contract_rows(left_qkv[:, rows], d_qkv[t]),
                    contract_rows(left_output[:, rows], attended[t]),
                ],
                axis=1,
            ).astype(jnp.bfloat16)
            for rows in (slice(0, half), slice(half, width))
        ]
        for t in range(sides)
    ]
    sum_attn = reduce_near(grad_attn)

    d_qkv, hidden_act = lax.optimization_barrier((d_qkv, hidden_act))
    branch_mlp = sum(contract_last(hidden_act[t], full_down[t]) for t in range(sides))
    branch_total = branch_attn + branch_mlp
    updated = input_float + gate[:, None] * branch_total
    block_output = place(block_input, updated.astype(jnp.bfloat16), own_index)
    d_logit = gate * (1.0 - gate) * jnp.sum(cot_rows * branch_total, axis=-1)

    d_normed_attn = sum(contract_last(d_qkv[t], full_qkv[t]) for t in range(sides))
    _, norm_back_attn = jax.vjp(rms_norm, input_float, attn_gain_f)
    d_input_norm, d_attn_gain = norm_back_attn(d_normed_attn)
    d_router = jnp.sum(d_logit[:, None] * input_float, axis=0)
    routed_grad = cot_rows + d_logit[:, None] * router_f + d_middle + d_input_norm
    block_grad = place(output_cot, routed_grad.astype(jnp.bfloat16), own_index)

    totals = sum_everywhere(jnp.stack([d_attn_gain, d_mlp_gain, d_router]))
    own = lax.dynamic_slice_in_dim(totals, rank * share, share, axis=1)
    return (
        block_output,
        block_grad,
        sum_attn[:, :heads],
        sum_attn[:, heads : 2 * heads],
        sum_attn[:, 2 * heads : 3 * heads],
        sum_attn[:, 3 * heads :],
        sum_up,
        sum_down,
        own[0],
        own[1],
        own[2],
    )


def solution(mesh):
    fine = Mesh(mesh.devices.reshape(-1, 2, mesh.shape["tensor"]), ("chips", "core", "tensor"))
    token = P(("chips", "core", "tensor"), None)
    weight = P(DP, "tensor")
    in_specs = (token, token, P(DP, None), P(DP, None)) + (weight,) * 6 + (P(DP),) * 3
    out_specs = (token, token) + (weight,) * 6 + (P(DP),) * 3
    return jax.shard_map(block, mesh=fine, in_specs=in_specs, out_specs=out_specs, check_vma=False)
```

```python
from functools import partial

import jax
import jax.numpy as jnp
from jax import lax
from jax.experimental import pallas as pl
from jax.experimental.pallas import tpu as pltpu
from jax.sharding import Mesh
from jax.sharding import PartitionSpec as P


HEAD_DIM = 64
EPSILON = 1e-05
DOCS = 16
PAIR = 2 * HEAD_DIM
DP = ("chips", "core")
ALL = ("tensor", "chips", "core")
SAME_CORE = ("tensor", "chips")


def rms_norm(values, gain):
    scale = lax.rsqrt(jnp.mean(values * values, axis=-1, keepdims=True) + EPSILON)
    return values * scale * gain


def plain_dot(left, right):
    return jnp.dot(left, right, preferred_element_type=jnp.float32)


def contract_rows(left, right):
    return lax.dot_general(
        left, right, (((0,), (0,)), ((), ())), preferred_element_type=jnp.float32
    )


def contract_last(left, right):
    return lax.dot_general(
        left, right, (((1,), (1,)), ((), ())), preferred_element_type=jnp.float32
    )


def fill_bias(seg_row_ref, seg_column_ref, bias_ref):
    rows = bias_ref.shape[0]
    key_at = lax.broadcasted_iota(jnp.int32, (rows, rows), 0)
    query_at = lax.broadcasted_iota(jnp.int32, (rows, rows), 1)
    same = seg_column_ref[...] == seg_row_ref[...]
    bias_ref[...] = jnp.where(same & (key_at <= query_at), 0.0, -1e30)


def lanes_of(head):
    lane = lax.broadcasted_iota(jnp.int32, (1, PAIR), 1)
    return (lane // HEAD_DIM == head).astype(jnp.bfloat16)


def attend(qkv, seg_row, seg_column):
    rows, width = qkv.shape[0], qkv.shape[1] // 3
    pairs = width // PAIR
    block = rows // 2
    scale = HEAD_DIM ** (-0.5)

    def kernel(seg_row_ref, seg_column_ref, q_ref, k_ref, v_ref, out_ref, lse_ref, bias_ref):
        @pl.when(pl.program_id(0) == 0)
        def _():
            fill_bias(seg_row_ref, seg_column_ref, bias_ref)

        query, keyed, valued = q_ref[...], k_ref[...], v_ref[...]
        lane = lax.broadcasted_iota(jnp.int32, (1, PAIR), 1)
        for low in range(0, rows, block):
            high = low + block
            found = []
            for head in (0, 1):
                chosen = query[low:high] * (lanes_of(head) * scale).astype(jnp.bfloat16)
                scores = contract_last(keyed[:high], chosen) + bias_ref[:high, low:high]
                top = jnp.max(scores, axis=0, keepdims=True)
                expanded = jnp.exp(scores - top)
                total = jnp.sum(expanded, axis=0, keepdims=True)
                lse_ref[head, :, low:high] = top + jnp.log(total)
                probs = (expanded * (1.0 / total)).astype(jnp.bfloat16)
                found.append(contract_rows(probs, valued[:high]))
            out_ref[low:high, :] = jnp.where(lane < HEAD_DIM, found[0], found[1]).astype(jnp.bfloat16)

    return pl.pallas_call(
        kernel,
        grid=(pairs,),
        out_shape=[
            jax.ShapeDtypeStruct((rows, width), jnp.bfloat16),
            jax.ShapeDtypeStruct((2 * pairs, 1, rows), jnp.float32),
        ],
        in_specs=[
            pl.BlockSpec((1, rows), lambda j: (0, 0)),
            pl.BlockSpec((rows, 1), lambda j: (0, 0)),
            pl.BlockSpec((rows, PAIR), lambda j: (0, j)),
            pl.BlockSpec((rows, PAIR), lambda j: (0, pairs + j)),
            pl.BlockSpec((rows, PAIR), lambda j: (0, 2 * pairs + j)),
        ],
        out_specs=[
            pl.BlockSpec((rows, PAIR), lambda j: (0, j)),
            pl.BlockSpec((2, 1, rows), lambda j: (j, 0, 0)),
        ],
        scratch_shapes=[pltpu.VMEM((rows, rows), jnp.float32)],
        name="attend",
    )(seg_row, seg_column, qkv, qkv, qkv)


def attend_back(qkv, d_attended, lse, seg_row, seg_column):
    rows, width = qkv.shape[0], qkv.shape[1] // 3
    pairs = width // PAIR
    block = rows // 2
    scale = HEAD_DIM ** (-0.5)

    def kernel(seg_row_ref, seg_column_ref, q_ref, k_ref, v_ref, d_ref, lse_ref, out_ref, bias_ref):
        step = pl.program_id(0)

        @pl.when(step == 0)
        def _():
            fill_bias(seg_row_ref, seg_column_ref, bias_ref)

        query, keyed, valued, d_out = q_ref[...], k_ref[...], v_ref[...], d_ref[...]
        scaled = query * jnp.bfloat16(scale)
        lane = lax.broadcasted_iota(jnp.int32, (1, PAIR), 1)
        first = lane < HEAD_DIM

        def store(at, low, high, pair):
            column = pl.multiple_of(at * width + step * PAIR, PAIR)
            out_ref[low:high, pl.ds(column, PAIR)] = jnp.where(first, pair[0], pair[1]).astype(jnp.bfloat16)

        d_key, d_value = [None, None], [None, None]
        for low in reversed(range(0, rows, block)):
            high = low + block
            d_query = []
            for head in (0, 1):
                lanes = lanes_of(head)
                scores = contract_last(keyed[:high], scaled[low:high] * lanes) + bias_ref[:high, low:high]
                probs = jnp.exp(scores - lse_ref[head, :, low:high])
                d_probs = contract_last(valued[:high], d_out[low:high] * lanes)
                inner = jnp.sum(probs * d_probs, axis=0, keepdims=True)
                d_scores = (probs * (d_probs - inner)).astype(jnp.bfloat16)
                more_value = plain_dot(probs.astype(jnp.bfloat16), d_out[low:high])
                more_key = plain_dot(d_scores, scaled[low:high])
                d_query.append(contract_rows(d_scores, keyed[:high]) * scale)
                if d_key[head] is not None:
                    more_value = more_value + d_value[head][:high]
                    more_key = more_key + d_key[head][:high]
                d_value[head], d_key[head] = more_value, more_key
            store(0, low, high, d_query)
            store(1, low, high, [part[low:] for part in d_key])
            store(2, low, high, [part[low:] for part in d_value])

    return pl.pallas_call(
        kernel,
        grid=(pairs,),
        out_shape=jax.ShapeDtypeStruct((rows, 3 * width), jnp.bfloat16),
        in_specs=[
            pl.BlockSpec((1, rows), lambda j: (0, 0)),
            pl.BlockSpec((rows, 1), lambda j: (0, 0)),
            pl.BlockSpec((rows, PAIR), lambda j: (0, j)),
            pl.BlockSpec((rows, PAIR), lambda j: (0, pairs + j)),
            pl.BlockSpec((rows, PAIR), lambda j: (0, 2 * pairs + j)),
            pl.BlockSpec((rows, PAIR), lambda j: (0, j)),
            pl.BlockSpec((2, 1, rows), lambda j: (j, 0, 0)),
        ],
        out_specs=pl.BlockSpec((rows, 3 * width), lambda j: (0, 0)),
        scratch_shapes=[pltpu.VMEM((rows, rows), jnp.float32)],
        name="attend_back",
    )(seg_row, seg_column, qkv, qkv, qkv, d_attended, lse)


def side_by_side(parts):
    columns = [part.shape[1] for part in parts]

    def kernel(*refs):
        at = 0
        for ref, count in zip(refs[:-1], columns):
            refs[-1][:, at : at + count] = ref[...]
            at += count

    shape = jax.ShapeDtypeStruct((parts[0].shape[0], sum(columns)), parts[0].dtype)
    return pl.pallas_call(kernel, out_shape=shape, name="side_by_side")(*parts)


def swap_cores(values):
    return lax.ppermute(values, "core", [(0, 1), (1, 0)])


def reduce_near(parts):
    kept = jnp.stack([part[0] for part in parts])
    got = swap_cores(jnp.stack([part[1] for part in parts]))
    total = (kept.astype(jnp.float32) + got.astype(jnp.float32)).astype(jnp.bfloat16)
    total = total.reshape(-1, total.shape[-1])
    return lax.psum_scatter(total, SAME_CORE, scatter_dimension=0, tiled=True).astype(jnp.float32)


def relative_order(values, near_only):
    width = values.shape[1]
    chips = lax.axis_size("chips")
    chip, core = lax.axis_index("chips"), lax.axis_index("core")
    share = width // (2 * chips)
    column = lax.broadcasted_iota(jnp.int32, (width, width), 1)
    row = lax.broadcasted_iota(jnp.int32, (width, width), 0)
    core_at = (column // (width // 2)) ^ core
    if near_only:
        chip_at = (column // share) % chips
    else:
        cross_at = (column // (width // 4)) % 2
        line_at = (column // share) % (chips // 2)
        chip_at = (line_at * 2 + cross_at) ^ chip
    wanted = (chip_at * 2 + core_at) * share + column % share
    return plain_dot(values, (row == wanted).astype(jnp.bfloat16)).astype(jnp.bfloat16)


def swap_sides(values):
    return lax.ppermute(values, "tensor", [(0, 1), (1, 0)])


def swap_chips(values, bit):
    return lax.ppermute(values, "chips", [(i, i ^ bit) for i in range(lax.axis_size("chips"))])


def add_low(left, right):
    return (left.astype(jnp.float32) + right.astype(jnp.float32)).astype(jnp.bfloat16)


def halve_line(values):
    bit = lax.axis_size("chips") // 2
    while bit > 1:
        half = values.shape[0] // 2
        got = swap_chips(values[half:], bit)
        values = values[:half].astype(jnp.float32) + got.astype(jnp.float32)
        bit //= 2
        if bit > 1:
            values = values.astype(jnp.bfloat16)
    return values


def halve_grads(left, right):
    half, columns = left.shape[1] // 2, right[0].shape[1]
    quarter = half // 2
    colors = (slice(0, columns // 2), slice(columns // 2, columns))
    sent = [contract_rows(left[:, half:], right[t]).astype(jnp.bfloat16) for t in (0, 1)]
    got = [swap_cores(sent[t]) for t in (0, 1)]
    part_a, part_b = [
        [add_low(contract_rows(left[:, :half], right[t][:, color]), got[t][:, color]) for t in (0, 1)]
        for color in colors
    ]
    got_a = swap_sides(part_a[1])
    got_b = [swap_chips(part_b[t][quarter:], 1) for t in (0, 1)]
    part_a = add_low(part_a[0], got_a)
    part_b = [add_low(part_b[t][:quarter], got_b[t]) for t in (0, 1)]
    got_a = swap_chips(part_a[quarter:], 1)
    got_b = swap_sides(part_b[1])
    part_a = add_low(part_a[:quarter], got_a)
    part_b = add_low(part_b[0], got_b)
    return halve_line(jnp.concatenate([part_a, part_b], axis=1)), sent


def place(whole, rows, index):
    tokens, width = whole.shape
    count = rows.shape[0]
    step = 512

    def kernel(index_ref, whole_ref, rows_ref, out_ref):
        at = pl.program_id(0) * step + lax.broadcasted_iota(jnp.int32, (step, count), 0)
        hit = (at == index_ref[...]).astype(jnp.float32)
        routed = jnp.sum(hit, axis=1, keepdims=True) > 0.5
        found = plain_dot(hit.astype(jnp.bfloat16), rows_ref[...])
        out_ref[...] = jnp.where(routed, found, whole_ref[...].astype(jnp.float32)).astype(jnp.bfloat16)

    return pl.pallas_call(
        kernel,
        grid=(tokens // step,),
        out_shape=jax.ShapeDtypeStruct(whole.shape, whole.dtype),
        in_specs=[
            pl.BlockSpec((1, count), lambda i: (0, 0)),
            pl.BlockSpec((step, width), lambda i: (i, 0)),
            pl.BlockSpec((count, width), lambda i: (0, 0)),
        ],
        out_specs=pl.BlockSpec((step, width), lambda i: (i, 0)),
        name="place_rows",
    )(index[None, :], whole, rows)


def sum_everywhere(values):
    values = values + swap_cores(values)
    values = values + swap_chips(values, 1)
    values = values + swap_sides(values)
    bit = lax.axis_size("chips") // 2
    while bit > 1:
        values = values + swap_chips(values, bit)
        bit //= 2
    return values


def block(
    block_input,
    output_cot,
    segment_ids,
    routed_index,
    w_query,
    w_key,
    w_value,
    w_output,
    w_up,
    w_down,
    attn_gain,
    mlp_gain,
    router_w,
):
    side = lax.axis_index("tensor")
    sides = lax.axis_size("tensor")
    rank = lax.axis_index(DP)
    width = block_input.shape[1]
    share, heads = w_query.shape
    hidden = w_up.shape[1]

    vectors = jnp.stack([attn_gain, mlp_gain, router_w], axis=1)
    vectors = jnp.pad(vectors, ((0, 0), (0, 128 - 3)))
    near = side_by_side([w_query, w_key, w_value, w_output, w_up, vectors])
    near = lax.all_gather(near, ALL, axis=0, tiled=True).reshape(sides, width, -1)
    far = lax.all_gather(w_down, ALL, axis=0, tiled=True).reshape(sides, width, -1)
    full_qkv = [near[t, :, : 3 * heads] for t in range(sides)]
    full_output = [near[t, :, 3 * heads : 4 * heads] for t in range(sides)]
    full_up = [near[t, :, 4 * heads : 4 * heads + hidden] for t in range(sides)]
    full_down = [far[t] for t in range(sides)]
    small = near[0, :, 4 * heads + hidden : 4 * heads + hidden + 3].astype(jnp.float32).T
    attn_gain_f, mlp_gain_f, router_f = small[0], small[1], small[2]

    own_index = lax.dynamic_index_in_dim(routed_index, side, 0, keepdims=False)
    own_segments = lax.dynamic_index_in_dim(segment_ids, side, 0, keepdims=False)
    input_float = jnp.take(block_input, own_index, axis=0).astype(jnp.float32)
    cot_rows = jnp.take(output_cot, own_index, axis=0).astype(jnp.float32)
    firsts = jnp.sum(
        (own_segments[None, :] < jnp.arange(1, DOCS, dtype=jnp.int32)[:, None]).astype(jnp.int32), axis=1
    )
    seg_routed = jnp.sum((own_index[:, None] >= firsts[None, :]).astype(jnp.int32), axis=1)
    seg_row, seg_column = seg_routed[None, :], seg_routed[:, None]

    normed_attn = rms_norm(input_float, attn_gain_f).astype(jnp.bfloat16)
    gate = jax.nn.sigmoid(jnp.sum(input_float * router_f, axis=-1))
    d_branch = gate[:, None] * cot_rows
    d_mlp_low = d_branch.astype(jnp.bfloat16)

    qkv = [plain_dot(normed_attn, full_qkv[t]).astype(jnp.bfloat16) for t in range(sides)]
    attended, lse = zip(*[attend(qkv[t], seg_row, seg_column) for t in range(sides)])
    branch_attn = sum(contract_last(attended[t], full_output[t]) for t in range(sides))
    middle = input_float + branch_attn
    normed_mlp = rms_norm(middle, mlp_gain_f).astype(jnp.bfloat16)

    hidden_pre = [plain_dot(normed_mlp, full_up[t]) for t in range(sides)]
    hidden_act = [jax.nn.gelu(hidden_pre[t], approximate=True).astype(jnp.bfloat16) for t in range(sides)]
    own_act = [jnp.where(side == 0, hidden_act[t], hidden_act[1 - t]) for t in range(sides)]
    left_down = relative_order(d_mlp_low, False)
    slope = []
    for t in range(sides):
        _, gelu_back = jax.vjp(partial(jax.nn.gelu, approximate=True), hidden_pre[t])
        slope.append(gelu_back(jnp.ones_like(hidden_pre[t]))[0])
    slope, own_act = lax.optimization_barrier((slope, own_act))
    sum_down, _ = halve_grads(left_down, own_act)
    d_pre = []
    for t in range(sides):
        d_act = plain_dot(d_mlp_low, full_down[t])
        d_pre.append((d_act * slope[t]).astype(jnp.bfloat16))
    own_pre = [jnp.where(side == 0, d_pre[t], d_pre[1 - t]) for t in range(sides)]
    left_up = relative_order(normed_mlp, False)
    sum_up, sent_up = halve_grads(left_up, own_pre)
    d_pre, sent_up = lax.optimization_barrier((d_pre, sent_up))

    d_normed_mlp = sum(contract_last(d_pre[t], full_up[t]) for t in range(sides))
    _, norm_back_mlp = jax.vjp(rms_norm, middle, mlp_gain_f)
    d_middle, d_mlp_gain = norm_back_mlp(d_normed_mlp)
    d_attn_low = (d_branch + d_middle).astype(jnp.bfloat16)
    d_qkv = []
    for t in range(sides):
        d_attended = plain_dot(d_attn_low, full_output[t]).astype(jnp.bfloat16)
        d_qkv.append(attend_back(qkv[t], d_attended, lse[t], seg_row, seg_column))
    half = width // 2
    left_qkv = relative_order(normed_attn, True)
    left_output = relative_order(d_attn_low, True)
    grad_attn = [
        [
            jnp.concatenate(
                [
                    contract_rows(left_qkv[:, rows], d_qkv[t]),
                    contract_rows(left_output[:, rows], attended[t]),
                ],
                axis=1,
            ).astype(jnp.bfloat16)
            for rows in (slice(0, half), slice(half, width))
        ]
        for t in range(sides)
    ]
    sum_attn = reduce_near(grad_attn)

    d_qkv, hidden_act = lax.optimization_barrier((d_qkv, hidden_act))
    branch_mlp = sum(contract_last(hidden_act[t], full_down[t]) for t in range(sides))
    branch_total = branch_attn + branch_mlp
    updated = input_float + gate[:, None] * branch_total
    block_output = place(block_input, updated.astype(jnp.bfloat16), own_index)
    d_logit = gate * (1.0 - gate) * jnp.sum(cot_rows * branch_total, axis=-1)

    d_normed_attn = sum(contract_last(d_qkv[t], full_qkv[t]) for t in range(sides))
    _, norm_back_attn = jax.vjp(rms_norm, input_float, attn_gain_f)
    d_input_norm, d_attn_gain = norm_back_attn(d_normed_attn)
    d_router = jnp.sum(d_logit[:, None] * input_float, axis=0)
    routed_grad = cot_rows + d_logit[:, None] * router_f + d_middle + d_input_norm
    block_grad = place(output_cot, routed_grad.astype(jnp.bfloat16), own_index)

    totals = sum_everywhere(jnp.stack([d_attn_gain, d_mlp_gain, d_router]))
    own = lax.dynamic_slice_in_dim(totals, rank * share, share, axis=1)
    return (
        block_output,
        block_grad,
        sum_attn[:, :heads],
        sum_attn[:, heads : 2 * heads],
        sum_attn[:, 2 * heads : 3 * heads],
        sum_attn[:, 3 * heads :],
        sum_up,
        sum_down,
        own[0],
        own[1],
        own[2],
    )


def solution(mesh):
    fine = Mesh(mesh.devices.reshape(-1, 2, mesh.shape["tensor"]), ("chips", "core", "tensor"))
    token = P(("chips", "core", "tensor"), None)
    weight = P(DP, "tensor")
    in_specs = (token, token, P(DP, None), P(DP, None)) + (weight,) * 6 + (P(DP),) * 3
    out_specs = (token, token) + (weight,) * 6 + (P(DP),) * 3
    return jax.shard_map(block, mesh=fine, in_specs=in_specs, out_specs=out_specs, check_vma=False)
```

```python
from functools import partial

import jax
import jax.numpy as jnp
from jax import lax
from jax.experimental import pallas as pl
from jax.experimental.pallas import tpu as pltpu
from jax.sharding import Mesh
from jax.sharding import PartitionSpec as P


HEAD_DIM = 64
EPSILON = 1e-05
DOCS = 16
PAIR = 2 * HEAD_DIM
DP = ("chips", "core")
ALL = ("tensor", "chips", "core")
SAME_CORE = ("tensor", "chips")


def rms_norm(values, gain):
    scale = lax.rsqrt(jnp.mean(values * values, axis=-1, keepdims=True) + EPSILON)
    return values * scale * gain


def plain_dot(left, right):
    return jnp.dot(left, right, preferred_element_type=jnp.float32)


def contract_rows(left, right):
    return lax.dot_general(
        left, right, (((0,), (0,)), ((), ())), preferred_element_type=jnp.float32
    )


def contract_last(left, right):
    return lax.dot_general(
        left, right, (((1,), (1,)), ((), ())), preferred_element_type=jnp.float32
    )


def fill_bias(seg_row_ref, seg_column_ref, bias_ref):
    rows = bias_ref.shape[0]
    key_at = lax.broadcasted_iota(jnp.int32, (rows, rows), 0)
    query_at = lax.broadcasted_iota(jnp.int32, (rows, rows), 1)
    same = seg_column_ref[...] == seg_row_ref[...]
    bias_ref[...] = jnp.where(same & (key_at <= query_at), 0.0, -1e30)


def lanes_of(head):
    lane = lax.broadcasted_iota(jnp.int32, (1, PAIR), 1)
    return (lane // HEAD_DIM == head).astype(jnp.bfloat16)


def attend(qkv, seg_row, seg_column):
    rows, width = qkv.shape[0], qkv.shape[1] // 3
    pairs = width // PAIR
    scale = HEAD_DIM ** (-0.5)

    def kernel(seg_row_ref, seg_column_ref, q_ref, k_ref, v_ref, out_ref, lse_ref, bias_ref):
        @pl.when(pl.program_id(0) == 0)
        def _():
            fill_bias(seg_row_ref, seg_column_ref, bias_ref)

        query, keyed, valued = q_ref[...], k_ref[...], v_ref[...]
        found = []
        for head in (0, 1):
            chosen = query * (lanes_of(head) * scale).astype(jnp.bfloat16)
            scores = contract_last(keyed, chosen) + bias_ref[...]
            top = jnp.max(scores, axis=0, keepdims=True)
            expanded = jnp.exp(scores - top)
            total = jnp.sum(expanded, axis=0, keepdims=True)
            lse_ref[head, :, :] = top + jnp.log(total)
            probs = (expanded * (1.0 / total)).astype(jnp.bfloat16)
            found.append(contract_rows(probs, valued))
        lane = lax.broadcasted_iota(jnp.int32, (1, PAIR), 1)
        out_ref[...] = jnp.where(lane < HEAD_DIM, found[0], found[1]).astype(jnp.bfloat16)

    return pl.pallas_call(
        kernel,
        grid=(pairs,),
        out_shape=[
            jax.ShapeDtypeStruct((rows, width), jnp.bfloat16),
            jax.ShapeDtypeStruct((2 * pairs, 1, rows), jnp.float32),
        ],
        in_specs=[
            pl.BlockSpec((1, rows), lambda j: (0, 0)),
            pl.BlockSpec((rows, 1), lambda j: (0, 0)),
            pl.BlockSpec((rows, PAIR), lambda j: (0, j)),
            pl.BlockSpec((rows, PAIR), lambda j: (0, pairs + j)),
            pl.BlockSpec((rows, PAIR), lambda j: (0, 2 * pairs + j)),
        ],
        out_specs=[
            pl.BlockSpec((rows, PAIR), lambda j: (0, j)),
            pl.BlockSpec((2, 1, rows), lambda j: (j, 0, 0)),
        ],
        scratch_shapes=[pltpu.VMEM((rows, rows), jnp.float32)],
        name="attend",
    )(seg_row, seg_column, qkv, qkv, qkv)


def attend_back(qkv, d_attended, lse, seg_row, seg_column):
    rows, width = qkv.shape[0], qkv.shape[1] // 3
    pairs = width // PAIR
    scale = HEAD_DIM ** (-0.5)

    def kernel(seg_row_ref, seg_column_ref, q_ref, k_ref, v_ref, d_ref, lse_ref, out_ref, bias_ref):
        step = pl.program_id(0)

        @pl.when(step == 0)
        def _():
            fill_bias(seg_row_ref, seg_column_ref, bias_ref)

        query, keyed, valued, d_out = q_ref[...], k_ref[...], v_ref[...], d_ref[...]
        scaled = query * jnp.bfloat16(scale)
        d_query, d_key, d_value = [], [], []
        for head in (0, 1):
            lanes = lanes_of(head)
            scores = contract_last(keyed, scaled * lanes) + bias_ref[...]
            probs = jnp.exp(scores - lse_ref[head, :, :])
            d_probs = contract_last(valued, d_out * lanes)
            inner = jnp.sum(probs * d_probs, axis=0, keepdims=True)
            d_scores = (probs * (d_probs - inner)).astype(jnp.bfloat16)
            d_value.append(plain_dot(probs.astype(jnp.bfloat16), d_out))
            d_key.append(plain_dot(d_scores, scaled))
            d_query.append(contract_rows(d_scores, keyed) * scale)
        lane = lax.broadcasted_iota(jnp.int32, (1, PAIR), 1)
        for at, pair in enumerate((d_query, d_key, d_value)):
            column = pl.multiple_of(at * width + step * PAIR, PAIR)
            out_ref[:, pl.ds(column, PAIR)] = jnp.where(lane < HEAD_DIM, pair[0], pair[1]).astype(
                jnp.bfloat16
            )

    return pl.pallas_call(
        kernel,
        grid=(pairs,),
        out_shape=jax.ShapeDtypeStruct((rows, 3 * width), jnp.bfloat16),
        in_specs=[
            pl.BlockSpec((1, rows), lambda j: (0, 0)),
            pl.BlockSpec((rows, 1), lambda j: (0, 0)),
            pl.BlockSpec((rows, PAIR), lambda j: (0, j)),
            pl.BlockSpec((rows, PAIR), lambda j: (0, pairs + j)),
            pl.BlockSpec((rows, PAIR), lambda j: (0, 2 * pairs + j)),
            pl.BlockSpec((rows, PAIR), lambda j: (0, j)),
            pl.BlockSpec((2, 1, rows), lambda j: (j, 0, 0)),
        ],
        out_specs=pl.BlockSpec((rows, 3 * width), lambda j: (0, 0)),
        scratch_shapes=[pltpu.VMEM((rows, rows), jnp.float32)],
        name="attend_back",
    )(seg_row, seg_column, qkv, qkv, qkv, d_attended, lse)


def side_by_side(parts):
    columns = [part.shape[1] for part in parts]

    def kernel(*refs):
        at = 0
        for ref, count in zip(refs[:-1], columns):
            refs[-1][:, at : at + count] = ref[...]
            at += count

    shape = jax.ShapeDtypeStruct((parts[0].shape[0], sum(columns)), parts[0].dtype)
    return pl.pallas_call(kernel, out_shape=shape, name="side_by_side")(*parts)


def swap_cores(values):
    return lax.ppermute(values, "core", [(0, 1), (1, 0)])


def reduce_near(parts):
    kept = jnp.stack([part[0] for part in parts])
    got = swap_cores(jnp.stack([part[1] for part in parts]))
    total = (kept.astype(jnp.float32) + got.astype(jnp.float32)).astype(jnp.bfloat16)
    total = total.reshape(-1, total.shape[-1])
    return lax.psum_scatter(total, SAME_CORE, scatter_dimension=0, tiled=True).astype(jnp.float32)


def relative_order(values, near_only):
    width = values.shape[1]
    chips = lax.axis_size("chips")
    chip, core = lax.axis_index("chips"), lax.axis_index("core")
    share = width // (2 * chips)
    column = lax.broadcasted_iota(jnp.int32, (width, width), 1)
    row = lax.broadcasted_iota(jnp.int32, (width, width), 0)
    core_at = (column // (width // 2)) ^ core
    if near_only:
        chip_at = (column // share) % chips
    else:
        cross_at = (column // (width // 4)) % 2
        line_at = (column // share) % (chips // 2)
        chip_at = (line_at * 2 + cross_at) ^ chip
    wanted = (chip_at * 2 + core_at) * share + column % share
    return plain_dot(values, (row == wanted).astype(jnp.bfloat16)).astype(jnp.bfloat16)


def swap_sides(values):
    return lax.ppermute(values, "tensor", [(0, 1), (1, 0)])


def swap_chips(values, bit):
    return lax.ppermute(values, "chips", [(i, i ^ bit) for i in range(lax.axis_size("chips"))])


def add_low(left, right):
    return (left.astype(jnp.float32) + right.astype(jnp.float32)).astype(jnp.bfloat16)


def halve_line(values):
    bit = lax.axis_size("chips") // 2
    while bit > 1:
        half = values.shape[0] // 2
        got = swap_chips(values[half:], bit)
        values = values[:half].astype(jnp.float32) + got.astype(jnp.float32)
        bit //= 2
        if bit > 1:
            values = values.astype(jnp.bfloat16)
    return values


def halve_grads(left, right):
    half, columns = left.shape[1] // 2, right[0].shape[1]
    quarter = half // 2
    colors = (slice(0, columns // 2), slice(columns // 2, columns))
    sent = [contract_rows(left[:, half:], right[t]).astype(jnp.bfloat16) for t in (0, 1)]
    got = [swap_cores(sent[t]) for t in (0, 1)]
    part_a, part_b = [
        [add_low(contract_rows(left[:, :half], right[t][:, color]), got[t][:, color]) for t in (0, 1)]
        for color in colors
    ]
    got_a = swap_sides(part_a[1])
    got_b = [swap_chips(part_b[t][quarter:], 1) for t in (0, 1)]
    part_a = add_low(part_a[0], got_a)
    part_b = [add_low(part_b[t][:quarter], got_b[t]) for t in (0, 1)]
    got_a = swap_chips(part_a[quarter:], 1)
    got_b = swap_sides(part_b[1])
    return (part_a[:quarter], got_a, part_b[0], got_b), sent


def finish_grads(state):
    part_a, got_a, part_b, got_b = state
    return halve_line(jnp.concatenate([add_low(part_a, got_a), add_low(part_b, got_b)], axis=1))


def place(whole, rows, index):
    tokens, width = whole.shape
    count = rows.shape[0]
    step = 512

    def kernel(index_ref, whole_ref, rows_ref, out_ref):
        at = pl.program_id(0) * step + lax.broadcasted_iota(jnp.int32, (step, count), 0)
        hit = (at == index_ref[...]).astype(jnp.float32)
        routed = jnp.sum(hit, axis=1, keepdims=True) > 0.5
        found = plain_dot(hit.astype(jnp.bfloat16), rows_ref[...])
        out_ref[...] = jnp.where(routed, found, whole_ref[...].astype(jnp.float32)).astype(jnp.bfloat16)

    return pl.pallas_call(
        kernel,
        grid=(tokens // step,),
        out_shape=jax.ShapeDtypeStruct(whole.shape, whole.dtype),
        in_specs=[
            pl.BlockSpec((1, count), lambda i: (0, 0)),
            pl.BlockSpec((step, width), lambda i: (i, 0)),
            pl.BlockSpec((count, width), lambda i: (0, 0)),
        ],
        out_specs=pl.BlockSpec((step, width), lambda i: (i, 0)),
        name="place_rows",
    )(index[None, :], whole, rows)


def sum_everywhere(values):
    values = values + swap_cores(values)
    values = values + swap_chips(values, 1)
    values = values + swap_sides(values)
    bit = lax.axis_size("chips") // 2
    while bit > 1:
        values = values + swap_chips(values, bit)
        bit //= 2
    return values


def block(
    block_input,
    output_cot,
    segment_ids,
    routed_index,
    w_query,
    w_key,
    w_value,
    w_output,
    w_up,
    w_down,
    attn_gain,
    mlp_gain,
    router_w,
):
    side = lax.axis_index("tensor")
    sides = lax.axis_size("tensor")
    rank = lax.axis_index(DP)
    width = block_input.shape[1]
    share, heads = w_query.shape
    hidden = w_up.shape[1]

    vectors = jnp.stack([attn_gain, mlp_gain, router_w], axis=1)
    vectors = jnp.pad(vectors, ((0, 0), (0, 128 - 3)))
    near = side_by_side([w_query, w_key, w_value, w_output, w_up, vectors])
    near = lax.all_gather(near, ALL, axis=0, tiled=True).reshape(sides, width, -1)
    far = lax.all_gather(w_down, ALL, axis=0, tiled=True).reshape(sides, width, -1)
    full_qkv = [near[t, :, : 3 * heads] for t in range(sides)]
    full_output = [near[t, :, 3 * heads : 4 * heads] for t in range(sides)]
    full_up = [near[t, :, 4 * heads : 4 * heads + hidden] for t in range(sides)]
    full_down = [far[t] for t in range(sides)]
    small = near[0, :, 4 * heads + hidden : 4 * heads + hidden + 3].astype(jnp.float32).T
    attn_gain_f, mlp_gain_f, router_f = small[0], small[1], small[2]

    own_index = lax.dynamic_index_in_dim(routed_index, side, 0, keepdims=False)
    own_segments = lax.dynamic_index_in_dim(segment_ids, side, 0, keepdims=False)
    input_float = jnp.take(block_input, own_index, axis=0).astype(jnp.float32)
    cot_rows = jnp.take(output_cot, own_index, axis=0).astype(jnp.float32)
    firsts = jnp.sum(
        (own_segments[None, :] < jnp.arange(1, DOCS, dtype=jnp.int32)[:, None]).astype(jnp.int32), axis=1
    )
    seg_routed = jnp.sum((own_index[:, None] >= firsts[None, :]).astype(jnp.int32), axis=1)
    seg_row, seg_column = seg_routed[None, :], seg_routed[:, None]

    normed_attn = rms_norm(input_float, attn_gain_f).astype(jnp.bfloat16)
    gate = jax.nn.sigmoid(jnp.sum(input_float * router_f, axis=-1))
    d_branch = gate[:, None] * cot_rows
    d_mlp_low = d_branch.astype(jnp.bfloat16)

    qkv = [plain_dot(normed_attn, full_qkv[t]).astype(jnp.bfloat16) for t in range(sides)]
    attended, lse = zip(*[attend(qkv[t], seg_row, seg_column) for t in range(sides)])
    branch_attn = sum(contract_last(attended[t], full_output[t]) for t in range(sides))
    middle = input_float + branch_attn
    normed_mlp = rms_norm(middle, mlp_gain_f).astype(jnp.bfloat16)

    hidden_pre = [plain_dot(normed_mlp, full_up[t]) for t in range(sides)]
    hidden_act = [jax.nn.gelu(hidden_pre[t], approximate=True).astype(jnp.bfloat16) for t in range(sides)]
    own_act = [jnp.where(side == 0, hidden_act[t], hidden_act[1 - t]) for t in range(sides)]
    left_down = relative_order(d_mlp_low, False)
    slope = []
    for t in range(sides):
        _, gelu_back = jax.vjp(partial(jax.nn.gelu, approximate=True), hidden_pre[t])
        slope.append(gelu_back(jnp.ones_like(hidden_pre[t]))[0])
    slope, own_act = lax.optimization_barrier((slope, own_act))
    state_down, _ = halve_grads(left_down, own_act)
    d_pre = []
    for t in range(sides):
        d_act = plain_dot(d_mlp_low, full_down[t])
        d_pre.append((d_act * slope[t]).astype(jnp.bfloat16))
    own_pre = [jnp.where(side == 0, d_pre[t], d_pre[1 - t]) for t in range(sides)]
    left_up = relative_order(normed_mlp, False)
    state_up, sent_up = halve_grads(left_up, own_pre)
    d_pre, sent_up = lax.optimization_barrier((d_pre, sent_up))

    d_normed_mlp = sum(contract_last(d_pre[t], full_up[t]) for t in range(sides))
    _, norm_back_mlp = jax.vjp(rms_norm, middle, mlp_gain_f)
    d_middle, d_mlp_gain = norm_back_mlp(d_normed_mlp)
    d_attn_low = (d_branch + d_middle).astype(jnp.bfloat16)
    d_qkv = [None] * sides
    for t in reversed(range(sides)):
        d_attended = plain_dot(d_attn_low, full_output[t]).astype(jnp.bfloat16)
        d_qkv[t] = attend_back(qkv[t], d_attended, lse[t], seg_row, seg_column)
    state_down, _ = lax.optimization_barrier((state_down, d_qkv[-1]))
    sum_down = finish_grads(state_down)
    sum_up = finish_grads(state_up)
    half = width // 2
    left_qkv = relative_order(normed_attn, True)
    left_output = relative_order(d_attn_low, True)
    grad_attn = [
        [
            jnp.concatenate(
                [
                    contract_rows(left_qkv[:, rows], d_qkv[t]),
                    contract_rows(left_output[:, rows], attended[t]),
                ],
                axis=1,
            ).astype(jnp.bfloat16)
            for rows in (slice(0, half), slice(half, width))
        ]
        for t in range(sides)
    ]
    sum_attn = reduce_near(grad_attn)

    d_qkv, hidden_act = lax.optimization_barrier((d_qkv, hidden_act))
    branch_mlp = sum(contract_last(hidden_act[t], full_down[t]) for t in range(sides))
    branch_total = branch_attn + branch_mlp
    updated = input_float + gate[:, None] * branch_total
    block_output = place(block_input, updated.astype(jnp.bfloat16), own_index)
    d_logit = gate * (1.0 - gate) * jnp.sum(cot_rows * branch_total, axis=-1)

    d_normed_attn = sum(contract_last(d_qkv[t], full_qkv[t]) for t in range(sides))
    _, norm_back_attn = jax.vjp(rms_norm, input_float, attn_gain_f)
    d_input_norm, d_attn_gain = norm_back_attn(d_normed_attn)
    d_router = jnp.sum(d_logit[:, None] * input_float, axis=0)
    routed_grad = cot_rows + d_logit[:, None] * router_f + d_middle + d_input_norm
    block_grad = place(output_cot, routed_grad.astype(jnp.bfloat16), own_index)

    totals = sum_everywhere(jnp.stack([d_attn_gain, d_mlp_gain, d_router]))
    own = lax.dynamic_slice_in_dim(totals, rank * share, share, axis=1)
    return (
        block_output,
        block_grad,
        sum_attn[:, :heads],
        sum_attn[:, heads : 2 * heads],
        sum_attn[:, 2 * heads : 3 * heads],
        sum_attn[:, 3 * heads :],
        sum_up,
        sum_down,
        own[0],
        own[1],
        own[2],
    )


def solution(mesh):
    fine = Mesh(mesh.devices.reshape(-1, 2, mesh.shape["tensor"]), ("chips", "core", "tensor"))
    token = P(("chips", "core", "tensor"), None)
    weight = P(DP, "tensor")
    in_specs = (token, token, P(DP, None), P(DP, None)) + (weight,) * 6 + (P(DP),) * 3
    out_specs = (token, token) + (weight,) * 6 + (P(DP),) * 3
    return jax.shard_map(block, mesh=fine, in_specs=in_specs, out_specs=out_specs, check_vma=False)
```
